512 devices in a mesh: tm: 128 (over x, z, core), head: 4 (over y).
Axes of the slice: x: 4, y: 4, z: 16, core: 2. Of those that a mesh axis runs over, the one named last changes fastest.
Arguments:
- latent: bfloat16 [65536, 1024], P('tm', 'head'), may hold values from -6 to 6
- timestep: int32 [1], replicated, may hold values from 0 to 999
- in_gain: float32 [1024], replicated, may hold values from 0.1 to 1.9
- w_x: bfloat16 [1024, 2048], P(None, 'head'), may hold values from -0.1875 to 0.1875
- w_z: bfloat16 [1024, 2048], P(None, 'head'), may hold values from -0.1875 to 0.1875
- w_bc: bfloat16 [1024, 256], replicated, may hold values from -0.1875 to 0.1875
- w_dt: bfloat16 [1024, 32], P(None, 'head'), may hold values from -0.1875 to 0.1875
- conv_x: float32 [4, 2048], P(None, 'head'), may hold values from -3 to 3
- conv_bc: float32 [4, 256], replicated, may hold values from -3 to 3
- dt_bias: float32 [32], P('head'), may hold values from -1 to 0.5
- a_log: float32 [32], P('head'), may hold values from -13 to -1, as said below
- d_skip: float32 [32], P('head'), may hold values from 4 to 64
- norm_gain: float32 [2048], P('head'), may hold values from 0.1 to 1.9
- w_out: bfloat16 [2048, 1024], P('head'), may hold values from -0.125 to 0.125
- w_mix: bfloat16 [1024, 1024], P(None, 'head'), may hold values from -0.1875 to 0.1875
Outputs:
- denoised: bfloat16 [65536, 1024], P('tm', 'head')
The draws below stay inside these ranges and needn't reach their ends.
Inputs may be any that keep to these rules, and one draw needn't show every extreme that they name: `a_log`: the logarithm of each head's decay rate.
All inputs are finite; a program needn't handle non-finite values.
Results may differ from the reference program's by a relative error of at most 0.012.
Values may be sent and summed in bfloat16 or wider, within the bound.
A program may use at most 128 MiB of HBM per device.

```python
import math
import jax
import jax.numpy as jnp
from jax import lax

D = 1024
HEADS = 32
HEADDIM = 64
STATE = 128
BLOCK = 256
CONV = 4
INNER = 2048
TOKENS = 65536


def draw_a_log(key, part):
    key_pick = jax.random.fold_in(key, 11)
    key_slow = jax.random.fold_in(key, 12)
    key_fast = jax.random.fold_in(key, 13)
    share = 0.5
    pick = jax.random.uniform(key_pick, (HEADS,), jnp.float32) < share
    slow_rate = jax.random.uniform(key_slow, (HEADS,), jnp.float32, jnp.log(0.3), jnp.log(2.0)) - jnp.log(jnp.float32(TOKENS))
    fast_rate = jax.random.uniform(key_fast, (HEADS,), jnp.float32, jnp.log(0.05), jnp.log(0.2))
    return jnp.where(pick, slow_rate, fast_rate).astype(jnp.float32)


def levels(stream_key, shape, shards, least, largest):
    loudness, own = 1.0, jax.random.fold_in(stream_key, 6)
    for dim, shards_of in shards:
        heights = jnp.exp(jax.random.uniform(jax.random.fold_in(own, dim), (shards_of,), jnp.float32, least / len(shards), largest / len(shards)))
        loudness = loudness * jnp.repeat(heights, shape[dim] // shards_of).reshape([-1 if axis == dim else 1 for axis in range(len(shape))])
    return loudness


def normal_values(stream_key, dims, scale, most, cuts=(), kind=jnp.bfloat16):
    factor_of = levels(stream_key, dims, cuts, -0.22, 0.18) if cuts else 1.0
    array = jax.random.normal(stream_key, dims, jnp.float32) * scale * factor_of
    return jnp.minimum(jnp.maximum(array, -most), most).astype(kind)


def setup_inputs(seed: int = 0) -> dict:
    arg_keys = jax.random.split(jax.random.key(seed), 16)
    return {
        "latent": normal_values(arg_keys[0], (TOKENS, D), 1.0, 6.0, ((0, 128), (1, 4))),
        "timestep": jax.random.randint(arg_keys[1], (1,), 0, 1000).astype(jnp.int32),
        "in_gain": jnp.clip(1.0 + 0.18 * jax.random.normal(arg_keys[2], (D,), jnp.float32), 0.1, 1.9),
        "w_x": normal_values(arg_keys[3], (D, INNER), D ** -0.5, 0.1875, ((1, 4),)),
        "w_z": normal_values(arg_keys[4], (D, INNER), D ** -0.5, 0.1875, ((1, 4),)),
        "w_bc": normal_values(arg_keys[5], (D, 2 * STATE), D ** -0.5, 0.1875),
        "w_dt": normal_values(arg_keys[6], (D, HEADS), D ** -0.5, 0.1875, ((1, 4),)),
        "conv_x": normal_values(arg_keys[7], (CONV, INNER), CONV ** -0.5, 3.0, ((1, 4),), jnp.float32),
        "conv_bc": normal_values(arg_keys[8], (CONV, 2 * STATE), CONV ** -0.5, 3.0, (), jnp.float32),
        "dt_bias": jnp.clip(-1.0 + 1.5 * jax.random.uniform(arg_keys[9], (HEADS,), jnp.float32) ** levels(arg_keys[9], (HEADS,), ((0, 4),), -0.2, 0.2), -1.0, 0.5),
        "a_log": draw_a_log(jax.random.fold_in(arg_keys[15], 71), 0),
        "d_skip": jnp.clip(jnp.exp(math.log(64.0) - 2.7725887 * jax.random.uniform(arg_keys[11], (HEADS,), jnp.float32) ** levels(arg_keys[11], (HEADS,), ((0, 4),), -0.2, 0.2)), 4.0, 64.0),
        "norm_gain": jnp.clip(1.0 + 0.18 * jax.random.normal(arg_keys[12], (INNER,), jnp.float32), 0.1, 1.9),
        "w_out": normal_values(arg_keys[13], (INNER, D), INNER ** -0.5, 0.125, ((0, 4),)),
        "w_mix": normal_values(arg_keys[14], (D, D), D ** -0.5, 0.1875, ((1, 4),)),
    }


def sinusoid(timestep, width):
    half = width // 2
    freq = jnp.exp(-math.log(10000.0) * jnp.arange(half, dtype=jnp.float32) / half)
    angle = timestep.astype(jnp.float32)[0] * freq
    return jnp.concatenate([jnp.sin(angle), jnp.cos(angle)])

def causal_conv(rows, rim, kernel):
    padded = jnp.concatenate([rim, rows], axis=0)
    count = rows.shape[0]
    total = jnp.zeros(rows.shape, jnp.float32)
    for k in range(kernel.shape[0]):
        total = total + padded[k:k + count].astype(jnp.float32) * kernel[k]
    return jax.nn.silu(total).astype(jnp.bfloat16)

def block_terms(xa, bmat, cmat, dt, la):
    steps = xa.shape[0]
    cum = jnp.cumsum(la, axis=0)
    scores = jnp.dot(cmat, bmat.T, preferred_element_type=jnp.float32)
    rowid = lax.broadcasted_iota(jnp.int32, (steps, steps), 0)
    colid = lax.broadcasted_iota(jnp.int32, (steps, steps), 1)
    causal = rowid >= colid
    cumt = cum.T
    seg = cumt[:, :, None] - cumt[:, None, :]
    decay = jnp.exp(jnp.where(causal[None], seg, -jnp.inf))
    mixw = (scores[None] * decay * dt.T[:, None, :]).astype(jnp.bfloat16)
    ydiag = jnp.einsum('hij,jhp->ihp', mixw.astype(jnp.float32), xa.astype(jnp.float32))
    tail = jnp.exp(cum[-1][None, :] - cum) * dt
    bw = (bmat.astype(jnp.float32)[:, None, :] * tail[:, :, None]).astype(jnp.bfloat16)
    state = jnp.einsum('jhn,jhp->hnp', bw.astype(jnp.float32), xa.astype(jnp.float32))
    total = jnp.exp(cum[-1])
    return (ydiag, state, total, cum)

def block_output(ydiag, cum, cmat, hin, xa, d_skip):
    hb = hin.astype(jnp.bfloat16)
    yoff = jnp.einsum('in,hnp->ihp', cmat.astype(jnp.float32), hb.astype(jnp.float32)) * jnp.exp(cum)[:, :, None]
    return ydiag + yoff + d_skip[None, :, None] * xa.astype(jnp.float32)

def reference(latent, timestep, in_gain, w_x, w_z, w_bc, w_dt, conv_x, conv_bc, dt_bias, a_log, d_skip, norm_gain, w_out, w_mix):
    u = latent.astype(jnp.float32) + sinusoid(timestep, D)[None, :]
    normed = (u * lax.rsqrt(lax.optimization_barrier(jnp.mean(u * u, axis=1, keepdims=True)) + 1e-05) * in_gain).astype(jnp.bfloat16)
    xs = jnp.dot(normed, w_x, preferred_element_type=jnp.float32).astype(jnp.bfloat16)
    gate = jnp.dot(normed, w_z, preferred_element_type=jnp.float32).astype(jnp.bfloat16)
    bc = jnp.dot(normed, w_bc, preferred_element_type=jnp.float32).astype(jnp.bfloat16)
    dt_raw = jnp.dot(normed, w_dt, preferred_element_type=jnp.float32)
    width = CONV - 1
    xa = causal_conv(xs, jnp.zeros((width, xs.shape[1]), jnp.bfloat16), conv_x)
    bca = causal_conv(bc, jnp.zeros((width, bc.shape[1]), jnp.bfloat16), conv_bc)
    bmat = bca[:, :STATE]
    cmat = bca[:, STATE:]
    dt = jax.nn.softplus(dt_raw + dt_bias)
    la = dt * -jnp.exp(a_log)
    blocks = TOKENS // BLOCK
    xa4 = xa.reshape(blocks, BLOCK, HEADS, HEADDIM)
    b3 = bmat.reshape(blocks, BLOCK, STATE)
    c3 = cmat.reshape(blocks, BLOCK, STATE)
    dt3 = dt.reshape(blocks, BLOCK, HEADS)
    la3 = la.reshape(blocks, BLOCK, HEADS)

    def advance(carry, item):
        xa_c, b_c, c_c, dt_c, la_c = item
        ydiag, state, total, cum = block_terms(xa_c, b_c, c_c, dt_c, la_c)
        y_c = block_output(ydiag, cum, c_c, carry, xa_c, d_skip)
        return (carry * total[:, None, None] + state, y_c)
    start = jnp.zeros((HEADS, STATE, HEADDIM), jnp.float32)
    _, ys = lax.scan(advance, start, (xa4, b3, c3, dt3, la3))
    y = ys.reshape(TOKENS, INNER)
    gated = y * jax.nn.silu(gate.astype(jnp.float32))
    square = lax.optimization_barrier(jnp.sum(gated * gated, axis=1, keepdims=True))
    yn = (gated * lax.rsqrt(square / INNER + 1e-05) * norm_gain).astype(jnp.bfloat16)
    hidden = (u + jnp.dot(yn, w_out, preferred_element_type=jnp.float32)).astype(jnp.bfloat16)
    mixed = hidden.astype(jnp.float32) + jnp.dot(hidden, w_mix, preferred_element_type=jnp.float32)
    return mixed.astype(jnp.bfloat16)
```

```python
import functools
import math

import jax
import jax.numpy as jnp
from jax import lax
from jax.experimental import pallas as pl
from jax.experimental.pallas import tpu as pltpu
from jax.sharding import PartitionSpec as P

BLOCK = 256
RIM = 16
LINE = 32
MESH = pl.DeviceIdType.MESH
VMEM = pl.BlockSpec(memory_space=pltpu.VMEM)
DMA = pltpu.SemaphoreType.DMA


def remote(src, dst, send, recv, **device):
    return pltpu.make_async_remote_copy(
        src_ref=src, dst_ref=dst, send_sem=send, recv_sem=recv, device_id=device, device_id_type=MESH
    )


def greet(devices, count):
    barrier = pltpu.get_barrier_semaphore()
    for device in devices:
        pl.semaphore_signal(barrier, inc=1, device_id=device, device_id_type=MESH)
    pl.semaphore_wait(barrier, count)


def aligned(index, size):
    return pl.ds(pl.multiple_of(index * size, size), size)


def gather_kernel(tms, heads, lat, out, own_sem, send, recv, rim_send, rim_recv):
    tm, me = lax.axis_index("tm"), lax.axis_index("head")
    right, left = lax.rem(me + 1, heads), lax.rem(me + heads - 1, heads)
    later, earlier = lax.rem(tm + 1, tms), lax.rem(tm + tms - 1, tms)
    rows, width = lat.shape
    half = rows // 2
    greet(
        [{"head": left}, {"head": right}] + [{"tm": earlier, "head": h} for h in range(heads)],
        2 + heads,
    )
    top, bottom = pl.ds(RIM, half), pl.ds(RIM + half, half)
    mine, lefts, rights = aligned(me, width), aligned(left, width), aligned(right, width)

    def own(rows_out, start, sem, to):
        return remote(
            lat.at[pl.ds(start, half)], out.at[rows_out, mine], send.at[sem], recv.at[sem], head=to
        )

    copies = [
        own(top, 0, 0, right),
        own(bottom, half, 1, left),
        own(bottom, half, 2, right),
        own(top, 0, 3, left),
    ]
    for copy in copies[:2]:
        copy.start()
    rims = [
        remote(
            lat.at[pl.ds(rows - RIM, RIM)],
            out.at[pl.ds(0, RIM), mine],
            rim_send.at[h],
            rim_recv.at[me],
            tm=later,
            head=h,
        )
        for h in range(heads)
    ]
    for copy in rims:
        copy.start()
    for copy in copies[2:]:
        copy.start()
    keep = pltpu.make_async_copy(lat, out.at[pl.ds(RIM, rows), mine], own_sem)
    keep.start()
    onward = [
        remote(out.at[top, lefts], out.at[top, lefts], send.at[4], recv.at[4], head=right),
        remote(out.at[bottom, rights], out.at[bottom, rights], send.at[5], recv.at[5], head=left),
    ]
    for copy, following in zip(copies[:2], onward):
        copy.wait_recv()
        following.start()
    for copy in copies[2:] + onward:
        copy.wait_recv()
    for h in range(heads):
        remote(
            lat.at[pl.ds(rows - RIM, RIM)],
            out.at[pl.ds(0, RIM), pl.ds(h * width, width)],
            rim_send.at[h],
            rim_recv.at[h],
            tm=later,
            head=h,
        ).wait_recv()
    for copy in copies + onward + rims:
        copy.wait_send()
    keep.wait()


def gather(lat, tms, heads):
    rows, width = lat.shape
    return pl.pallas_call(
        functools.partial(gather_kernel, tms, heads),
        out_shape=jax.ShapeDtypeStruct((rows + RIM, width * heads), lat.dtype),
        in_specs=[VMEM],
        out_specs=VMEM,
        scratch_shapes=[DMA, DMA((6,)), DMA((6,)), DMA((heads,)), DMA((heads,))],
        compiler_params=pltpu.CompilerParams(collective_id=0, has_side_effects=True),
        name="gather_rows",
    )(lat)


def scan_kernel(
    line, lines, piece, s, g, out, sin, gin, pre, dec, back, xt, xd, s_sem, g_sem, xt_sem, xd_sem, b_sem
):
    tm = lax.axis_index("tm")
    me, mine = lax.rem(tm, line), tm // line
    base = mine * line
    high, wide = piece
    stack = s.shape[0] // high

    def rows(k):
        return aligned(lax.rem(k, stack), high)

    def cols(k):
        return aligned(k // stack, wide)

    barrier = pltpu.get_barrier_semaphore()

    def other(o):
        return lax.rem(me + o, line)

    def other_line(o):
        return lax.rem(mine + o, lines)

    @pl.loop(1, line)
    def _(o):
        pl.semaphore_signal(barrier, inc=1, device_id={"tm": base + other(o)}, device_id_type=MESH)

    for o in range(1, lines):
        pl.semaphore_signal(
            barrier, inc=1, device_id={"tm": other_line(o) * line + me}, device_id_type=MESH
        )
    pl.semaphore_wait(barrier, line - 1 + lines - 1)

    def out_s(q):
        return remote(s.at[rows(q), cols(q)], sin.at[me], s_sem.at[0, q], s_sem.at[1, me], tm=base + q)

    def out_g(q):
        return remote(g.at[:, cols(q)], gin.at[me], g_sem.at[0, q], g_sem.at[1, me], tm=base + q)

    def in_s(q):
        return remote(s.at[rows(q), cols(q)], sin.at[q], s_sem.at[0, q], s_sem.at[1, q], tm=base + q)

    def in_g(q):
        return remote(g.at[:, cols(q)], gin.at[q], g_sem.at[0, q], g_sem.at[1, q], tm=base + q)

    @pl.loop(1, line)
    def _(o):
        q = other(o)
        out_g(q).start()
        out_s(q).start()

    sin[me] = s[rows(me), cols(me)]
    gin[me] = g[:, cols(me)]

    def step(k, carry):
        state, decay = carry

        @pl.when(k != me)
        def _():
            in_g(k).wait_recv()
            in_s(k).wait_recv()

        pre[k] = state
        dec[k] = decay
        factor = gin[k]
        return state * factor + sin[k].astype(jnp.float32), decay * factor

    state, decay = lax.fori_loop(
        0, line, step, (jnp.zeros((high, wide), jnp.float32), jnp.ones((1, wide), jnp.float32))
    )
    xt[mine] = state
    xd[mine] = decay

    def line_copies(q, slot):
        device = q * line + me
        return (
            remote(xt.at[slot], xt.at[slot], xt_sem.at[0, q], xt_sem.at[1, slot], tm=device),
            remote(xd.at[slot], xd.at[slot], xd_sem.at[0, q], xd_sem.at[1, slot], tm=device),
        )

    for o in range(1, lines):
        for copy in line_copies(other_line(o), mine):
            copy.start()
    for o in range(1, lines):
        for copy in line_copies(other_line(o), other_line(o)):
            copy.wait_recv()
    start = jnp.zeros((high, wide), jnp.float32)
    for k in range(lines):
        start = jnp.where(k < mine, start * xd[k] + xt[k], start)

    def final(k, carry):
        back[k] = (start * dec[k] + pre[k]).astype(back.dtype)
        return carry

    lax.fori_loop(0, line, final, 0)

    def out_b(q):
        return remote(
            back.at[q], out.at[rows(me), cols(me)], b_sem.at[0, q], b_sem.at[1, me], tm=base + q
        )

    def in_b(q):
        return remote(
            back.at[q], out.at[rows(q), cols(q)], b_sem.at[0, q], b_sem.at[1, q], tm=base + q
        )

    @pl.loop(1, line)
    def _(o):
        out_b(other(o)).start()

    out[rows(me), cols(me)] = back[me]

    for o in range(1, lines):
        for copy in line_copies(other_line(o), mine):
            copy.wait_send()

    @pl.loop(1, line)
    def _(o):
        q = other(o)
        out_g(q).wait_send()
        out_s(q).wait_send()
        in_b(q).wait_recv()
        out_b(q).wait_send()


def scan_states(s, g, tms):
    line = min(LINE, tms)
    lines = tms // line
    high, wide = 16, 128
    while (s.shape[0] // high) * (s.shape[1] // wide) > line:
        if wide < s.shape[1]:
            wide *= 2
        else:
            high *= 2
    f32 = jnp.float32
    return pl.pallas_call(
        functools.partial(scan_kernel, line, lines, (high, wide)),
        out_shape=jax.ShapeDtypeStruct(s.shape, s.dtype),
        in_specs=[VMEM, VMEM],
        out_specs=VMEM,
        scratch_shapes=[
            pltpu.VMEM((line, high, wide), s.dtype),
            pltpu.VMEM((line, 1, wide), f32),
            pltpu.VMEM((line, high, wide), f32),
            pltpu.VMEM((line, 1, wide), f32),
            pltpu.VMEM((line, high, wide), s.dtype),
            pltpu.VMEM((lines, high, wide), f32),
            pltpu.VMEM((lines, 1, wide), f32),
            DMA((2, line)),
            DMA((2, line)),
            DMA((2, lines)),
            DMA((2, lines)),
            DMA((2, line)),
        ],
        compiler_params=pltpu.CompilerParams(collective_id=1, has_side_effects=True),
        name="scan_states",
    )(s, g)


def mix_kernel(heads, inner, part, sq, u, w_mix, out, hid, first, full, stage, sqs, send, recv, sq_sem):
    me = lax.axis_index("head")
    right, left, across = (lax.rem(me + d, heads) for d in (1, heads - 1, 2))
    share = u.shape[0]
    half = share // 2
    width = w_mix.shape[1]
    greet([{"head": left}, {"head": right}, {"head": across}], 3)

    def halves(k):
        start = pl.multiple_of(k * share, share)
        return pl.ds(start, half), pl.ds(pl.multiple_of(start + half, half), half)

    top, bottom = pl.ds(0, half), pl.ds(half, half)
    right_top, right_bottom = halves(right)
    left_top, left_bottom = halves(left)
    across_top, across_bottom = halves(across)

    def go(n, src, dst, to):
        return remote(src, dst, send.at[n], recv.at[n], head=to)

    one = [
        go(0, part.at[across_top], first.at[0], right),
        go(1, part.at[across_bottom], first.at[1], left),
        go(2, part.at[right_bottom], full.at[0, bottom], right),
        go(3, part.at[left_top], full.at[1, top], left),
    ]
    for copy in one:
        copy.start()

    def sq_copy(to, slot):
        return remote(sq.at[to], sqs.at[slot], sq_sem.at[0, to], sq_sem.at[1, slot], head=to)

    for to in (right, left, across):
        sq_copy(to, me).start()
    sqs[me] = sq[me]
    two = [
        go(4, stage.at[0], full.at[0, top], right),
        go(5, stage.at[1], full.at[1, bottom], left),
    ]
    for n, rows in ((0, right_top), (1, left_bottom)):
        one[n].wait_recv()
        stage[n] = (part[rows].astype(jnp.float32) + first[n].astype(jnp.float32)).astype(stage.dtype)
        two[n].start()
    for frm in (right, left, across):
        sq_copy(frm, frm).wait_recv()
    square = sqs[0]
    for k in range(1, heads):
        square = square + sqs[k]
    scale = lax.rsqrt(jnp.broadcast_to(square, (share, share)).T / inner + 1e-05)
    for copy in one[2:] + two:
        copy.wait_recv()
    own = aligned(me, share)
    for k in range(u.shape[1] // share):
        cols = pl.ds(k * share, share)
        total = part[own, cols].astype(jnp.float32)
        total = total + full[0, :, cols].astype(jnp.float32) + full[1, :, cols].astype(jnp.float32)
        hid[own, cols] = (u[:, cols] + scale * total).astype(hid.dtype)
    own_top, own_bottom = halves(me)
    three = [
        go(6, hid.at[own_top], hid.at[own_top], right),
        go(7, hid.at[own_bottom], hid.at[own_bottom], left),
        go(8, hid.at[own_bottom], hid.at[own_bottom], right),
        go(9, hid.at[own_top], hid.at[own_top], left),
    ]
    for copy in three:
        copy.start()
    four = [
        go(10, hid.at[left_top], hid.at[left_top], right),
        go(11, hid.at[right_bottom], hid.at[right_bottom], left),
    ]
    mine = aligned(me, width)

    def finish(k):
        rows = aligned(k, share)
        mixed = jnp.dot(hid[rows], w_mix[...], preferred_element_type=jnp.float32)
        out[rows] = (hid[rows, mine].astype(jnp.float32) + mixed).astype(out.dtype)

    for copy, following in zip(three[:2], four):
        copy.wait_recv()
        following.start()
    finish(me)
    for copy in three[2:]:
        copy.wait_recv()
    finish(left)
    finish(right)
    for copy in four:
        copy.wait_recv()
    finish(across)
    for copy in one + two + three + four:
        copy.wait_send()
    for to in (right, left, across):
        sq_copy(to, me).wait_send()


def mix(part, sq, u, w_mix, heads, inner):
    rows, width = part.shape
    share = rows // heads
    bf16 = jnp.bfloat16
    return pl.pallas_call(
        functools.partial(mix_kernel, heads, inner),
        out_shape=jax.ShapeDtypeStruct((rows, w_mix.shape[1]), bf16),
        in_specs=[VMEM] * 4,
        out_specs=VMEM,
        scratch_shapes=[
            pltpu.VMEM((rows, width), bf16),
            pltpu.VMEM((2, share // 2, width), bf16),
            pltpu.VMEM((2, share, width), bf16),
            pltpu.VMEM((2, share // 2, width), bf16),
            pltpu.VMEM((heads, 1, share), jnp.float32),
            DMA((12,)),
            DMA((12,)),
            DMA((2, heads)),
        ],
        compiler_params=pltpu.CompilerParams(collective_id=2, has_side_effects=True),
        name="mix_rows",
    )(part, sq, u, w_mix)


def sinusoid(timestep, width):
    half = width // 2
    freq = jnp.exp(-math.log(10000.0) * jnp.arange(half, dtype=jnp.float32) / half)
    angle = timestep.astype(jnp.float32)[0] * freq
    return jnp.concatenate([jnp.sin(angle), jnp.cos(angle)])


def causal_conv(rows, kernel):
    width = kernel.shape[0]
    count = rows.shape[0] - RIM
    first = RIM - width + 1
    total = jnp.zeros((count, rows.shape[1]), jnp.float32)
    for k in range(width):
        total = total + rows[first + k : first + k + count].astype(jnp.float32) * kernel[k]
    return jax.nn.silu(total).astype(jnp.bfloat16)


def spread(per_head, hdim):
    return jnp.repeat(per_head, hdim, axis=-1)


def diagonal(xa, bmat, cmat, dt, cum):
    steps = xa.shape[0]
    scores = jnp.dot(cmat, bmat.T, preferred_element_type=jnp.float32)
    rowid = lax.broadcasted_iota(jnp.int32, (steps, steps), 0)
    colid = lax.broadcasted_iota(jnp.int32, (steps, steps), 1)
    causal = rowid >= colid
    cumt = cum.T
    seg = cumt[:, :, None] - cumt[:, None, :]
    decay = jnp.exp(jnp.where(causal[None], seg, -jnp.inf))
    mixw = (scores[None] * decay * dt.T[:, None, :]).astype(jnp.bfloat16)
    return jnp.einsum("hij,jhp->ihp", mixw, xa, preferred_element_type=jnp.float32)


def shards(
    latent,
    timestep,
    in_gain,
    w_x,
    w_z,
    w_bc,
    w_dt,
    conv_x,
    conv_bc,
    dt_bias,
    a_log,
    d_skip,
    norm_gain,
    w_out,
    w_mix,
):
    f32, bf16 = jnp.float32, jnp.bfloat16
    tms, devices = lax.axis_size("tm"), lax.axis_size("head")
    whole = gather(latent, tms, devices)
    emb = sinusoid(timestep, whole.shape[1])[None, :]
    u = whole.astype(f32) + emb
    normed = (u * lax.rsqrt(jnp.mean(u * u, axis=1, keepdims=True) + 1e-05) * in_gain).astype(bf16)
    xs = jnp.dot(normed, w_x, preferred_element_type=f32).astype(bf16)
    bc = jnp.dot(normed, w_bc, preferred_element_type=f32).astype(bf16)
    gate = jnp.dot(normed[RIM:], w_z, preferred_element_type=f32).astype(bf16)
    dt_raw = jnp.dot(normed[RIM:], w_dt, preferred_element_type=f32)
    inside = (lax.broadcasted_iota(jnp.int32, (xs.shape[0], 1), 0) >= RIM) | (lax.axis_index("tm") > 0)
    xa = causal_conv(jnp.where(inside, xs, 0), conv_x)
    bca = causal_conv(jnp.where(inside, bc, 0), conv_bc)
    state_n = w_bc.shape[1] // 2
    dt = jax.nn.softplus(dt_raw + dt_bias)
    la = dt * -jnp.exp(a_log)
    steps, heads = dt.shape
    hdim = xa.shape[1] // heads
    blocks = steps // BLOCK
    terms = []
    for b in range(blocks):
        rows = slice(b * BLOCK, (b + 1) * BLOCK)
        bmat, cmat = bca[rows, :state_n], bca[rows, state_n:]
        cum = jnp.cumsum(la[rows], axis=0)
        tail = jnp.exp(cum[-1:] - cum) * dt[rows]
        weighted = (xa[rows].astype(f32) * spread(tail, hdim)).astype(bf16)
        state = lax.dot_general(
            bmat, weighted, (((0,), (0,)), ((), ())), preferred_element_type=f32
        )
        total = spread(jnp.exp(cum[-1:]), hdim)
        terms.append((rows, bmat, cmat, cum, state, total))
    run_state, run_total = terms[0][4], terms[0][5]
    for term in terms[1:]:
        run_state, run_total = run_state * term[5] + term[4], run_total * term[5]
    incoming = scan_states(run_state.astype(bf16), run_total, tms).astype(f32)
    ys = []
    for rows, bmat, cmat, cum, state, total in terms:
        ydiag = diagonal(xa[rows].reshape(BLOCK, heads, hdim), bmat, cmat, dt[rows], cum)
        yoff = jnp.dot(cmat, incoming.astype(bf16), preferred_element_type=f32)
        ys.append(ydiag.reshape(BLOCK, heads * hdim) + yoff * spread(jnp.exp(cum), hdim))
        incoming = incoming * total + state
    y = jnp.concatenate(ys, axis=0) + spread(d_skip[None, :], hdim) * xa.astype(f32)
    gated = y * jax.nn.silu(gate.astype(f32))
    share = steps // devices
    square = jnp.sum(gated * gated, axis=1).reshape(devices, 1, share)
    scaled = (gated * norm_gain).astype(bf16)
    part = jnp.dot(scaled, w_out, preferred_element_type=f32).astype(bf16)
    own = lax.dynamic_slice_in_dim(whole, RIM + lax.axis_index("head") * share, share, 0)
    inner = gated.shape[1] * devices
    return mix(part, square, own.astype(f32) + emb, w_mix, devices, inner)


def solution(mesh):
    in_specs = (
        P("tm", "head"),
        P(),
        P(),
        P(None, "head"),
        P(None, "head"),
        P(),
        P(None, "head"),
        P(None, "head"),
        P(),
        P("head"),
        P("head"),
        P("head"),
        P("head"),
        P("head", None),
        P(None, "head"),
    )
    out_specs = P("tm", "head")
    return jax.shard_map(shards, mesh=mesh, in_specs=in_specs, out_specs=out_specs, check_vma=False)
```

```python
import functools
import math

import jax
import jax.numpy as jnp
from jax import lax
from jax.experimental import pallas as pl
from jax.experimental.pallas import tpu as pltpu
from jax.sharding import PartitionSpec as P

BLOCK = 256
RIM = 16
LINE = 32
MESH = pl.DeviceIdType.MESH
VMEM = pl.BlockSpec(memory_space=pltpu.VMEM)
DMA = pltpu.SemaphoreType.DMA


def remote(src, dst, send, recv, **device):
    return pltpu.make_async_remote_copy(
        src_ref=src, dst_ref=dst, send_sem=send, recv_sem=recv, device_id=device, device_id_type=MESH
    )


def greet(devices, count):
    barrier = pltpu.get_barrier_semaphore()
    for device in devices:
        pl.semaphore_signal(barrier, inc=1, device_id=device, device_id_type=MESH)
    pl.semaphore_wait(barrier, count)


def aligned(index, size):
    return pl.ds(pl.multiple_of(index * size, size), size)


def gather_kernel(tms, heads, lat, out, own_sem, send, recv, rim_send, rim_recv):
    tm, me = lax.axis_index("tm"), lax.axis_index("head")
    right, left = lax.rem(me + 1, heads), lax.rem(me + heads - 1, heads)
    later, earlier = lax.rem(tm + 1, tms), lax.rem(tm + tms - 1, tms)
    rows, width = lat.shape
    half = rows // 2
    greet(
        [{"head": left}, {"head": right}] + [{"tm": earlier, "head": h} for h in range(heads)],
        2 + heads,
    )
    top, bottom = pl.ds(RIM, half), pl.ds(RIM + half, half)
    mine, lefts, rights = aligned(me, width), aligned(left, width), aligned(right, width)

    def own(rows_out, start, sem, to):
        return remote(
            lat.at[pl.ds(start, half)], out.at[rows_out, mine], send.at[sem], recv.at[sem], head=to
        )

    copies = [
        own(top, 0, 0, right),
        own(bottom, half, 1, left),
        own(bottom, half, 2, right),
        own(top, 0, 3, left),
    ]
    for copy in copies[:2]:
        copy.start()
    rims = [
        remote(
            lat.at[pl.ds(rows - RIM, RIM)],
            out.at[pl.ds(0, RIM), mine],
            rim_send.at[h],
            rim_recv.at[me],
            tm=later,
            head=h,
        )
        for h in range(heads)
    ]
    for copy in rims:
        copy.start()
    for copy in copies[2:]:
        copy.start()
    keep = pltpu.make_async_copy(lat, out.at[pl.ds(RIM, rows), mine], own_sem)
    keep.start()
    onward = [
        remote(out.at[top, lefts], out.at[top, lefts], send.at[4], recv.at[4], head=right),
        remote(out.at[bottom, rights], out.at[bottom, rights], send.at[5], recv.at[5], head=left),
    ]
    for copy, following in zip(copies[:2], onward):
        copy.wait_recv()
        following.start()
    for copy in copies[2:] + onward:
        copy.wait_recv()
    for h in range(heads):
        remote(
            lat.at[pl.ds(rows - RIM, RIM)],
            out.at[pl.ds(0, RIM), pl.ds(h * width, width)],
            rim_send.at[h],
            rim_recv.at[h],
            tm=later,
            head=h,
        ).wait_recv()
    for copy in copies + onward + rims:
        copy.wait_send()
    keep.wait()


def gather(lat, tms, heads):
    rows, width = lat.shape
    return pl.pallas_call(
        functools.partial(gather_kernel, tms, heads),
        out_shape=jax.ShapeDtypeStruct((rows + RIM, width * heads), lat.dtype),
        in_specs=[VMEM],
        out_specs=VMEM,
        scratch_shapes=[DMA, DMA((6,)), DMA((6,)), DMA((heads,)), DMA((heads,))],
        compiler_params=pltpu.CompilerParams(collective_id=0, has_side_effects=True),
        name="gather_rows",
    )(lat)


def split(value):
    parts = []
    for _ in range(3):
        part = value.astype(jnp.bfloat16)
        parts.append(part)
        value = value - part.astype(jnp.float32)
    return parts


def exact(value, ones):
    total = None
    for part in split(value):
        term = jnp.dot(part, ones, preferred_element_type=jnp.float32)
        total = term if total is None else total + term
    return total


def iota(shape, axis):
    return lax.broadcasted_iota(jnp.int32, shape, axis)


def column(row):
    count = row.shape[1]
    wide = jnp.broadcast_to(row, (count, count))
    return jnp.sum(
        jnp.where(iota((count, count), 0) == iota((count, count), 1), wide, 0.0), axis=1, keepdims=True
    )


def layer_kernel(
    tms,
    line,
    piece,
    devices,
    whole,
    emb,
    in_gain,
    w_x,
    w_z,
    w_bc,
    w_dt,
    conv_x,
    conv_bc,
    dt_bias,
    a_log,
    d_skip,
    norm_gain,
    w_out,
    w_mix,
    out,
    nrm,
    xs,
    bcs,
    xa,
    bb,
    cc,
    cums,
    dts,
    cols_t,
    ec,
    states,
    totals,
    s,
    g,
    yd,
    z,
    hin,
    hb,
    part,
    sq,
    sin,
    gin,
    pre,
    dec,
    back,
    xt,
    xd,
    hid,
    first,
    full,
    stage,
    sqs,
    s_sem,
    g_sem,
    xt_sem,
    xd_sem,
    b_sem,
    send,
    recv,
    sq_sem,
):
    f32, bf16 = jnp.float32, jnp.bfloat16
    lines = tms // line
    tm = lax.axis_index("tm")
    here, mine = lax.rem(tm, line), tm // line
    base = mine * line
    high, wide = piece
    stack = s.shape[0] // high
    me = lax.axis_index("head")
    right, left, across = (lax.rem(me + d, devices) for d in (1, devices - 1, 2))

    def rows(k):
        return aligned(lax.rem(k, stack), high)

    def cols(k):
        return aligned(k // stack, wide)

    def other(o):
        return lax.rem(here + o, line)

    def other_line(o):
        return lax.rem(mine + o, lines)

    barrier = pltpu.get_barrier_semaphore()

    @pl.loop(1, line)
    def _(o):
        pl.semaphore_signal(barrier, inc=1, device_id={"tm": base + other(o)}, device_id_type=MESH)

    for o in range(1, lines):
        pl.semaphore_signal(
            barrier, inc=1, device_id={"tm": other_line(o) * line + here}, device_id_type=MESH
        )
    for device in (left, right, across):
        pl.semaphore_signal(barrier, inc=1, device_id={"head": device}, device_id_type=MESH)

    total_rows = whole.shape[0]
    steps = total_rows - RIM
    chunk = total_rows // 11

    @pl.loop(0, 11)
    def _(c):
        at = aligned(c, chunk)
        u = whole[at].astype(f32) + emb[...]
        mean = jnp.mean(u * u, axis=1, keepdims=True)
        nrm[at] = (u * lax.rsqrt(mean + 1e-05) * in_gain[...]).astype(bf16)

    dt_t = lax.dot_general(
        w_dt[...], nrm[RIM:], (((1,), (1,)), ((), ())), preferred_element_type=f32
    )
    xs[...] = jnp.dot(nrm[...], w_x[...], preferred_element_type=f32).astype(bf16).astype(f32)
    bcs[...] = jnp.dot(nrm[...], w_bc[...], preferred_element_type=f32).astype(bf16).astype(f32)

    @pl.when(tm == 0)
    def _():
        xs[:RIM] = jnp.zeros((RIM, xs.shape[1]), f32)
        bcs[:RIM] = jnp.zeros((RIM, bcs.shape[1]), f32)

    taps = conv_x.shape[0]
    state_n = bb.shape[1]
    width = 128

    def conv(source, kernel, c, lanes):
        value = source[pl.ds(pl.multiple_of(c * width + RIM - 8, 8), width + 8), lanes]
        total = jnp.zeros((width, value.shape[1]), f32)
        for k in range(taps):
            at = 8 - taps + 1 + k
            total = total + value[at : at + width] * kernel[k : k + 1, lanes]
        return jax.nn.silu(total).astype(bf16)

    @pl.loop(0, steps // width)
    def _(c):
        at = aligned(c, width)
        for lane in range(0, xs.shape[1], 128):
            lanes = pl.ds(lane, 128)
            xa[at, lanes] = conv(xs, conv_x, c, lanes)
        bb[at] = conv(bcs, conv_bc, c, pl.ds(0, state_n))
        cc[at] = conv(bcs, conv_bc, c, pl.ds(state_n, state_n))

    raw = dt_t + column(dt_bias[...])
    dt_t = jnp.maximum(raw, 0.0) + jnp.log1p(jnp.exp(-jnp.abs(raw)))
    la_t = dt_t * -jnp.exp(column(a_log[...]))
    heads = dt_t.shape[0]
    channels = xa.shape[1]
    hdim = channels // heads
    blocks = steps // BLOCK
    upper = jnp.where(iota((BLOCK, BLOCK), 0) <= iota((BLOCK, BLOCK), 1), 1.0, 0.0).astype(bf16)

    def picks(offset):
        hit = iota((128, channels), 0) == iota((128, channels), 1) // hdim + offset
        return jnp.where(hit, 1.0, 0.0).astype(bf16)

    tail_picks, decay_picks = picks(heads), picks(2 * heads)
    for b in range(blocks):
        span = slice(b * BLOCK, (b + 1) * BLOCK)
        dt_b = dt_t[:, span]
        cum_b = exact(la_t[:, span], upper)
        last = cum_b[:, BLOCK - 1 :]
        tail = jnp.exp(last - cum_b) * dt_b
        cums[b] = cum_b
        dts[b] = dt_b
        pad = jnp.zeros((128 - 3 * heads, BLOCK), f32)
        columns = jnp.concatenate([cum_b, tail, jnp.exp(cum_b), pad], axis=0).T
        cols_t[span] = columns
        ec[span] = exact(columns, decay_picks)
        weighted = (xa[span].astype(f32) * exact(columns, tail_picks)).astype(bf16)
        states[b] = jnp.dot(
            bb[span].astype(f32).T.astype(bf16), weighted, preferred_element_type=f32
        )
        totals[b] = ec[(b + 1) * BLOCK - 1 : (b + 1) * BLOCK]
    run_state, run_total = states[0], totals[0]
    for b in range(1, blocks):
        run_state, run_total = run_state * totals[b] + states[b], run_total * totals[b]
    s[...] = run_state.astype(bf16)
    g[...] = run_total
    pl.semaphore_wait(barrier, line - 1 + lines - 1 + 3)

    def out_s(q):
        return remote(s.at[rows(q), cols(q)], sin.at[here], s_sem.at[0, q], s_sem.at[1, here], tm=base + q)

    def out_g(q):
        return remote(g.at[:, cols(q)], gin.at[here], g_sem.at[0, q], g_sem.at[1, here], tm=base + q)

    def in_s(q):
        return remote(s.at[rows(q), cols(q)], sin.at[q], s_sem.at[0, q], s_sem.at[1, q], tm=base + q)

    def in_g(q):
        return remote(g.at[:, cols(q)], gin.at[q], g_sem.at[0, q], g_sem.at[1, q], tm=base + q)

    @pl.loop(1, line)
    def _(o):
        q = other(o)
        out_g(q).start()
        out_s(q).start()

    sin[here] = s[rows(here), cols(here)]
    gin[here] = g[:, cols(here)]

    def diagonal(b):
        at = aligned(b, BLOCK)
        scores = lax.dot_general(
            cc[at], bb[at], (((1,), (1,)), ((), ())), preferred_element_type=f32
        )
        causal = iota((BLOCK, BLOCK), 0) >= iota((BLOCK, BLOCK), 1)
        cols_b, cum_b, dt_b = cols_t[at], cums[b], dts[b]
        per = 128 // hdim
        for first_head in range(0, heads, per):
            lanes = slice(first_head * hdim, (first_head + per) * hdim)
            xa_b = xa[at, lanes]
            lane = iota((BLOCK, 128), 1) // hdim
            total = jnp.zeros((BLOCK, 128), f32)
            for i in range(per):
                h = first_head + i
                seg = jnp.where(causal, cols_b[:, h : h + 1] - cum_b[h : h + 1], -jnp.inf)
                mixw = (scores * jnp.exp(seg) * dt_b[h : h + 1]).astype(bf16)
                product = jnp.dot(mixw, xa_b, preferred_element_type=f32)
                total = jnp.where(lane == i, product, total)
            yd[at, lanes] = total

    diagonal(0)

    def step(k, carry):
        state, decay = carry

        @pl.when(k != here)
        def _():
            in_g(k).wait_recv()
            in_s(k).wait_recv()

        pre[k] = state
        dec[k] = decay
        factor = gin[k]
        return state * factor + sin[k].astype(f32), decay * factor

    state, decay = lax.fori_loop(
        0, line, step, (jnp.zeros((high, wide), f32), jnp.ones((1, wide), f32))
    )
    xt[mine] = state
    xd[mine] = decay

    def line_copies(q, slot):
        device = q * line + here
        return (
            remote(xt.at[slot], xt.at[slot], xt_sem.at[0, q], xt_sem.at[1, slot], tm=device),
            remote(xd.at[slot], xd.at[slot], xd_sem.at[0, q], xd_sem.at[1, slot], tm=device),
        )

    for o in range(1, lines):
        for copy in line_copies(other_line(o), mine):
            copy.start()
    z[...] = jax.nn.silu(
        jnp.dot(nrm[RIM:], w_z[...], preferred_element_type=f32).astype(bf16).astype(f32)
    )
    for o in range(1, lines):
        for copy in line_copies(other_line(o), other_line(o)):
            copy.wait_recv()
    start = jnp.zeros((high, wide), f32)
    for k in range(lines):
        start = jnp.where(k < mine, start * xd[k] + xt[k], start)

    def final(k, carry):
        back[k] = (start * dec[k] + pre[k]).astype(back.dtype)
        return carry

    lax.fori_loop(0, line, final, 0)

    def out_b(q):
        return remote(
            back.at[q], hin.at[rows(here), cols(here)], b_sem.at[0, q], b_sem.at[1, here], tm=base + q
        )

    def in_b(q):
        return remote(
            back.at[q], hin.at[rows(q), cols(q)], b_sem.at[0, q], b_sem.at[1, q], tm=base + q
        )

    @pl.loop(1, line)
    def _(o):
        out_b(other(o)).start()

    hin[rows(here), cols(here)] = back[here]
    for b in range(1, blocks):
        diagonal(b)

    @pl.loop(1, line)
    def _(o):
        in_b(other(o)).wait_recv()

    incoming = hin[...].astype(f32)
    for b in range(blocks):
        hb[b] = incoming.astype(bf16)
        incoming = incoming * totals[b] + states[b]

    share = steps // devices
    half = share // 2
    inner = channels * devices
    hit = iota((heads, channels), 0) == iota((heads, channels), 1) // hdim
    skip = jnp.sum(jnp.where(hit, column(d_skip[...]), 0.0), axis=0, keepdims=True)

    def product(k):
        at = aligned(k, share)
        yoff = jnp.dot(cc[at], hb[k * share // BLOCK], preferred_element_type=f32)
        y = yd[at] + yoff * ec[at] + skip * xa[at].astype(f32)
        gated = y * z[at]
        square = jnp.sum(gated * gated, axis=1, keepdims=True)
        sq[k] = jnp.broadcast_to(square, (share, share)).T[:1]
        scaled = (gated * norm_gain[...]).astype(bf16)
        part[at] = jnp.dot(scaled, w_out[...], preferred_element_type=f32).astype(bf16)

    def halves(k):
        begin = pl.multiple_of(k * share, share)
        return pl.ds(begin, half), pl.ds(pl.multiple_of(begin + half, half), half)

    top, bottom = pl.ds(0, half), pl.ds(half, half)
    right_top, right_bottom = halves(right)
    left_top, left_bottom = halves(left)
    across_top, across_bottom = halves(across)

    def go(n, src, dst, to):
        return remote(src, dst, send.at[n], recv.at[n], head=to)

    one = [
        go(0, part.at[across_top], first.at[0], right),
        go(1, part.at[across_bottom], first.at[1], left),
        go(2, part.at[right_bottom], full.at[0, bottom], right),
        go(3, part.at[left_top], full.at[1, top], left),
    ]

    def sq_copy(to, slot):
        return remote(sq.at[to], sqs.at[slot], sq_sem.at[0, to], sq_sem.at[1, slot], head=to)

    product(across)
    product(right)
    one[0].start()
    one[1].start()
    product(left)
    one[2].start()
    product(me)
    one[3].start()
    for to in (right, left, across):
        sq_copy(to, me).start()
    sqs[me] = sq[me]
    two = [
        go(4, stage.at[0], full.at[0, top], right),
        go(5, stage.at[1], full.at[1, bottom], left),
    ]
    for n, at in ((0, right_top), (1, left_bottom)):
        one[n].wait_recv()
        stage[n] = (part[at].astype(f32) + first[n].astype(f32)).astype(stage.dtype)
        two[n].start()
    for frm in (right, left, across):
        sq_copy(frm, frm).wait_recv()
    square = sqs[0]
    for k in range(1, devices):
        square = square + sqs[k]
    scale = lax.rsqrt(jnp.broadcast_to(square, (share, share)).T / inner + 1e-05)
    for copy in one[2:] + two:
        copy.wait_recv()
    own = aligned(me, share)
    own_rim = pl.ds(pl.multiple_of(me * share + RIM, RIM), share)
    for k in range(whole.shape[1] // share):
        at = pl.ds(k * share, share)
        total = part[own, at].astype(f32)
        total = total + full[0, :, at].astype(f32) + full[1, :, at].astype(f32)
        u = whole[own_rim, at].astype(f32) + emb[:, at]
        hid[own, at] = (u + scale * total).astype(hid.dtype)
    own_top, own_bottom = halves(me)
    three = [
        go(6, hid.at[own_top], hid.at[own_top], right),
        go(7, hid.at[own_bottom], hid.at[own_bottom], left),
        go(8, hid.at[own_bottom], hid.at[own_bottom], right),
        go(9, hid.at[own_top], hid.at[own_top], left),
    ]
    for copy in three:
        copy.start()
    four = [
        go(10, hid.at[left_top], hid.at[left_top], right),
        go(11, hid.at[right_bottom], hid.at[right_bottom], left),
    ]
    mix_cols = aligned(me, w_mix.shape[1])

    def finish(k):
        at = aligned(k, share)
        mixed = jnp.dot(hid[at], w_mix[...], preferred_element_type=f32)
        out[at] = (hid[at, mix_cols].astype(f32) + mixed).astype(out.dtype)

    for copy, following in zip(three[:2], four):
        copy.wait_recv()
        following.start()
    finish(me)
    for copy in three[2:]:
        copy.wait_recv()
    finish(left)
    finish(right)
    for copy in four:
        copy.wait_recv()
    finish(across)
    for copy in one + two + three + four:
        copy.wait_send()
    for to in (right, left, across):
        sq_copy(to, me).wait_send()
    for o in range(1, lines):
        for copy in line_copies(other_line(o), mine):
            copy.wait_send()

    @pl.loop(1, line)
    def _(o):
        q = other(o)
        out_g(q).wait_send()
        out_s(q).wait_send()
        out_b(q).wait_send()


def layer(tms, devices, whole, emb, in_gain, w_x, w_z, w_bc, w_dt, *rest):
    f32, bf16 = jnp.float32, jnp.bfloat16
    w_mix = rest[-1]
    rows, features = whole.shape
    steps, channels, state_n = rows - RIM, w_x.shape[1], w_bc.shape[1] // 2
    heads = w_dt.shape[0]
    blocks = steps // BLOCK
    share = steps // devices
    line = min(LINE, tms)
    lines = tms // line
    high, wide = 16, 128
    while (state_n // high) * (channels // wide) > line:
        if wide < channels:
            wide *= 2
        else:
            high *= 2
    scratch = [
        ((rows, features), bf16),
        ((rows, channels), f32),
        ((rows, 2 * state_n), f32),
        ((steps, channels), bf16),
        ((steps, state_n), bf16),
        ((steps, state_n), bf16),
        ((blocks, heads, BLOCK), f32),
        ((blocks, heads, BLOCK), f32),
        ((steps, 128), f32),
        ((steps, channels), f32),
        ((blocks, state_n, channels), f32),
        ((blocks, 1, channels), f32),
        ((state_n, channels), bf16),
        ((1, channels), f32),
        ((steps, channels), f32),
        ((steps, channels), f32),
        ((state_n, channels), bf16),
        ((blocks, state_n, channels), bf16),
        ((steps, features), bf16),
        ((devices, 1, share), f32),
        ((line, high, wide), bf16),
        ((line, 1, wide), f32),
        ((line, high, wide), f32),
        ((line, 1, wide), f32),
        ((line, high, wide), bf16),
        ((lines, high, wide), f32),
        ((lines, 1, wide), f32),
        ((steps, features), bf16),
        ((2, share // 2, features), bf16),
        ((2, share, features), bf16),
        ((2, share // 2, features), bf16),
        ((devices, 1, share), f32),
    ]
    args = (whole, emb, in_gain, w_x, w_z, w_bc, w_dt) + rest
    return pl.pallas_call(
        functools.partial(layer_kernel, tms, line, (high, wide), devices),
        out_shape=jax.ShapeDtypeStruct((steps, w_mix.shape[1]), bf16),
        in_specs=[VMEM] * len(args),
        out_specs=VMEM,
        scratch_shapes=[pltpu.VMEM(shape, kind) for shape, kind in scratch]
        + [
            DMA((2, line)),
            DMA((2, line)),
            DMA((2, lines)),
            DMA((2, lines)),
            DMA((2, line)),
            DMA((12,)),
            DMA((12,)),
            DMA((2, devices)),
        ],
        compiler_params=pltpu.CompilerParams(collective_id=1, has_side_effects=True),
        name="layer",
    )(*args)


def sinusoid(timestep, width):
    half = width // 2
    freq = jnp.exp(-math.log(10000.0) * jnp.arange(half, dtype=jnp.float32) / half)
    angle = timestep.astype(jnp.float32)[0] * freq
    return jnp.concatenate([jnp.sin(angle), jnp.cos(angle)])


def shards(
    latent,
    timestep,
    in_gain,
    w_x,
    w_z,
    w_bc,
    w_dt,
    conv_x,
    conv_bc,
    dt_bias,
    a_log,
    d_skip,
    norm_gain,
    w_out,
    w_mix,
):
    tms, devices = lax.axis_size("tm"), lax.axis_size("head")
    whole = gather(latent, tms, devices)
    return layer(
        tms,
        devices,
        whole,
        sinusoid(timestep, whole.shape[1])[None, :],
        in_gain[None, :],
        w_x,
        w_z,
        w_bc,
        w_dt.T,
        conv_x,
        conv_bc,
        dt_bias[None, :],
        a_log[None, :],
        d_skip[None, :],
        norm_gain[None, :],
        w_out,
        w_mix,
    )


def solution(mesh):
    in_specs = (
        P("tm", "head"),
        P(),
        P(),
        P(None, "head"),
        P(None, "head"),
        P(),
        P(None, "head"),
        P(None, "head"),
        P(),
        P("head"),
        P("head"),
        P("head"),
        P("head"),
        P("head", None),
        P(None, "head"),
    )
    out_specs = P("tm", "head")
    return jax.shard_map(shards, mesh=mesh, in_specs=in_specs, out_specs=out_specs, check_vma=False)
```

```python
import functools
import math

import jax
import jax.numpy as jnp
from jax import lax
from jax.experimental import pallas as pl
from jax.experimental.pallas import tpu as pltpu
from jax.sharding import PartitionSpec as P

BLOCK = 256
RIM = 16
LINE = 32
MESH = pl.DeviceIdType.MESH
VMEM = pl.BlockSpec(memory_space=pltpu.VMEM)
FAR = pl.BlockSpec(memory_space=pl.ANY)
DMA = pltpu.SemaphoreType.DMA


def remote(src, dst, send, recv, **device):
    return pltpu.make_async_remote_copy(
        src_ref=src, dst_ref=dst, send_sem=send, recv_sem=recv, device_id=device, device_id_type=MESH
    )


def greet(devices, count):
    barrier = pltpu.get_barrier_semaphore()
    for device in devices:
        pl.semaphore_signal(barrier, inc=1, device_id=device, device_id_type=MESH)
    pl.semaphore_wait(barrier, count)


def aligned(index, size):
    return pl.ds(pl.multiple_of(index * size, size), size)


def gather_kernel(tms, heads, lat, out, own_sem, send, recv, rim_send, rim_recv):
    tm, me = lax.axis_index("tm"), lax.axis_index("head")
    right, left = lax.rem(me + 1, heads), lax.rem(me + heads - 1, heads)
    later, earlier = lax.rem(tm + 1, tms), lax.rem(tm + tms - 1, tms)
    rows, width = lat.shape
    half = rows // 2
    greet(
        [{"head": left}, {"head": right}] + [{"tm": earlier, "head": h} for h in range(heads)],
        2 + heads,
    )
    top, bottom = pl.ds(RIM, half), pl.ds(RIM + half, half)
    mine, lefts, rights = aligned(me, width), aligned(left, width), aligned(right, width)

    def own(rows_out, start, sem, to):
        return remote(
            lat.at[pl.ds(start, half)], out.at[rows_out, mine], send.at[sem], recv.at[sem], head=to
        )

    copies = [
        own(top, 0, 0, right),
        own(bottom, half, 1, left),
        own(bottom, half, 2, right),
        own(top, 0, 3, left),
    ]
    for copy in copies[:2]:
        copy.start()
    rims = [
        remote(
            lat.at[pl.ds(rows - RIM, RIM)],
            out.at[pl.ds(0, RIM), mine],
            rim_send.at[h],
            rim_recv.at[me],
            tm=later,
            head=h,
        )
        for h in range(heads)
    ]
    for copy in rims:
        copy.start()
    for copy in copies[2:]:
        copy.start()
    keep = pltpu.make_async_copy(lat, out.at[pl.ds(RIM, rows), mine], own_sem)
    keep.start()
    onward = [
        remote(out.at[top, lefts], out.at[top, lefts], send.at[4], recv.at[4], head=right),
        remote(out.at[bottom, rights], out.at[bottom, rights], send.at[5], recv.at[5], head=left),
    ]
    for copy, following in zip(copies[:2], onward):
        copy.wait_recv()
        following.start()
    for copy in copies[2:] + onward:
        copy.wait_recv()
    for h in range(heads):
        remote(
            lat.at[pl.ds(rows - RIM, RIM)],
            out.at[pl.ds(0, RIM), pl.ds(h * width, width)],
            rim_send.at[h],
            rim_recv.at[h],
            tm=later,
            head=h,
        ).wait_recv()
    for copy in copies + onward + rims:
        copy.wait_send()
    keep.wait()


def gather(lat, tms, heads):
    rows, width = lat.shape
    return pl.pallas_call(
        functools.partial(gather_kernel, tms, heads),
        out_shape=jax.ShapeDtypeStruct((rows + RIM, width * heads), lat.dtype),
        in_specs=[VMEM],
        out_specs=VMEM,
        scratch_shapes=[DMA, DMA((6,)), DMA((6,)), DMA((heads,)), DMA((heads,))],
        compiler_params=pltpu.CompilerParams(collective_id=0, has_side_effects=True),
        name="gather_rows",
    )(lat)


def split(value):
    parts = []
    for _ in range(3):
        part = value.astype(jnp.bfloat16)
        parts.append(part)
        value = value - part.astype(jnp.float32)
    return parts


def exact(value, ones):
    total = None
    for part in split(value):
        term = jnp.dot(part, ones, preferred_element_type=jnp.float32)
        total = term if total is None else total + term
    return total


def iota(shape, axis):
    return lax.broadcasted_iota(jnp.int32, shape, axis)


def column(row):
    count = row.shape[1]
    wide = jnp.broadcast_to(row, (count, count))
    return jnp.sum(
        jnp.where(iota((count, count), 0) == iota((count, count), 1), wide, 0.0), axis=1, keepdims=True
    )


def layer_kernel(
    tms,
    line,
    piece,
    devices,
    whole,
    emb,
    in_gain,
    w_x_far,
    w_z_far,
    w_bc_far,
    w_dt,
    conv_x,
    conv_bc,
    dt_bias,
    a_log,
    d_skip,
    norm_gain,
    w_out_far,
    w_mix_far,
    out,
    w_x,
    w_z,
    w_bc,
    w_out,
    w_mix,
    nrm,
    xs,
    bcs,
    xa,
    bb,
    cc,
    cums,
    dts,
    cols_t,
    ec,
    states,
    totals,
    s,
    g,
    yd,
    z,
    hin,
    hb,
    part,
    sq,
    sin,
    gin,
    pre,
    dec,
    back,
    xt,
    xd,
    hid,
    first,
    full,
    stage,
    sqs,
    s_sem,
    g_sem,
    xt_sem,
    xd_sem,
    b_sem,
    send,
    recv,
    sq_sem,
    w_sem,
):
    f32, bf16 = jnp.float32, jnp.bfloat16
    lines = tms // line
    tm = lax.axis_index("tm")
    here, mine = lax.rem(tm, line), tm // line
    base = mine * line
    high, wide = piece
    stack = s.shape[0] // high
    me = lax.axis_index("head")
    right, left, across = (lax.rem(me + d, devices) for d in (1, devices - 1, 2))

    def rows(k):
        return aligned(lax.rem(k, stack), high)

    def cols(k):
        return aligned(k // stack, wide)

    def other(o):
        return lax.rem(here + o, line)

    def other_line(o):
        return lax.rem(mine + o, lines)

    def far_first(i):
        away = (i + 1) // 2
        return other(line // 2 + jnp.where(lax.rem(i, 2) == 0, away, -away))

    pairs = ((w_x_far, w_x), (w_bc_far, w_bc), (w_z_far, w_z), (w_out_far, w_out), (w_mix_far, w_mix))
    loads = [pltpu.make_async_copy(far, near, w_sem.at[n]) for n, (far, near) in enumerate(pairs)]
    for load in loads:
        load.start()
    barrier = pltpu.get_barrier_semaphore()

    @pl.loop(0, line - 1)
    def _(i):
        pl.semaphore_signal(barrier, inc=1, device_id={"tm": base + far_first(i)}, device_id_type=MESH)

    for o in range(1, lines):
        pl.semaphore_signal(
            barrier, inc=1, device_id={"tm": other_line(o) * line + here}, device_id_type=MESH
        )
    for device in (left, right, across):
        pl.semaphore_signal(barrier, inc=1, device_id={"head": device}, device_id_type=MESH)

    total_rows = whole.shape[0]
    steps = total_rows - RIM
    chunk = total_rows // 11

    @pl.loop(0, 11)
    def _(c):
        at = aligned(c, chunk)
        u = whole[at].astype(f32) + emb[...]
        mean = jnp.mean(u * u, axis=1, keepdims=True)
        nrm[at] = (u * lax.rsqrt(mean + 1e-05) * in_gain[...]).astype(bf16)

    dt_t = lax.dot_general(
        w_dt[...], nrm[RIM:], (((1,), (1,)), ((), ())), preferred_element_type=f32
    )
    loads[0].wait()
    xs[...] = jnp.dot(nrm[...], w_x[...], preferred_element_type=f32).astype(bf16).astype(f32)
    loads[1].wait()
    bcs[...] = jnp.dot(nrm[...], w_bc[...], preferred_element_type=f32).astype(bf16).astype(f32)

    @pl.when(tm == 0)
    def _():
        xs[:RIM] = jnp.zeros((RIM, xs.shape[1]), f32)
        bcs[:RIM] = jnp.zeros((RIM, bcs.shape[1]), f32)

    taps = conv_x.shape[0]
    state_n = bb.shape[1]
    width = 128

    def conv(source, kernel, c, lanes):
        value = source[pl.ds(pl.multiple_of(c * width + RIM - 8, 8), width + 8), lanes]
        total = jnp.zeros((width, value.shape[1]), f32)
        for k in range(taps):
            at = 8 - taps + 1 + k
            total = total + value[at : at + width] * kernel[k : k + 1, lanes]
        return jax.nn.silu(total).astype(bf16)

    @pl.loop(0, steps // width)
    def _(c):
        at = aligned(c, width)
        for lane in range(0, xs.shape[1], 128):
            lanes = pl.ds(lane, 128)
            xa[at, lanes] = conv(xs, conv_x, c, lanes)
        bb[at] = conv(bcs, conv_bc, c, pl.ds(0, state_n))
        cc[at] = conv(bcs, conv_bc, c, pl.ds(state_n, state_n))

    raw = dt_t + column(dt_bias[...])
    dt_t = jnp.maximum(raw, 0.0) + jnp.log1p(jnp.exp(-jnp.abs(raw)))
    la_t = dt_t * -jnp.exp(column(a_log[...]))
    heads = dt_t.shape[0]
    channels = xa.shape[1]
    hdim = channels // heads
    blocks = steps // BLOCK
    upper = jnp.where(iota((BLOCK, BLOCK), 0) <= iota((BLOCK, BLOCK), 1), 1.0, 0.0).astype(bf16)

    def picks(offset):
        hit = iota((128, channels), 0) == iota((128, channels), 1) // hdim + offset
        return jnp.where(hit, 1.0, 0.0).astype(bf16)

    tail_picks, decay_picks = picks(heads), picks(2 * heads)
    for b in range(blocks):
        span = slice(b * BLOCK, (b + 1) * BLOCK)
        dt_b = dt_t[:, span]
        cum_b = exact(la_t[:, span], upper)
        last = cum_b[:, BLOCK - 1 :]
        tail = jnp.exp(last - cum_b) * dt_b
        cums[b] = cum_b
        dts[b] = dt_b
        pad = jnp.zeros((128 - 3 * heads, BLOCK), f32)
        columns = jnp.concatenate([cum_b, tail, jnp.exp(cum_b), pad], axis=0).T
        cols_t[span] = columns
        ec[span] = exact(columns, decay_picks)
        weighted = (xa[span].astype(f32) * exact(columns, tail_picks)).astype(bf16)
        states[b] = jnp.dot(
            bb[span].astype(f32).T.astype(bf16), weighted, preferred_element_type=f32
        )
        totals[b] = ec[(b + 1) * BLOCK - 1 : (b + 1) * BLOCK]
    run_state, run_total = states[0], totals[0]
    for b in range(1, blocks):
        run_state, run_total = run_state * totals[b] + states[b], run_total * totals[b]
    s[...] = run_state.astype(bf16)
    g[...] = run_total
    pl.semaphore_wait(barrier, line - 1 + lines - 1 + 3)

    def out_s(q):
        return remote(s.at[rows(q), cols(q)], sin.at[here], s_sem.at[0, q], s_sem.at[1, here], tm=base + q)

    def out_g(q):
        return remote(g.at[:, cols(q)], gin.at[here], g_sem.at[0, q], g_sem.at[1, here], tm=base + q)

    def in_s(q):
        return remote(s.at[rows(q), cols(q)], sin.at[q], s_sem.at[0, q], s_sem.at[1, q], tm=base + q)

    def in_g(q):
        return remote(g.at[:, cols(q)], gin.at[q], g_sem.at[0, q], g_sem.at[1, q], tm=base + q)

    @pl.loop(0, line - 1)
    def _(i):
        q = far_first(i)
        out_g(q).start()
        out_s(q).start()

    sin[here] = s[rows(here), cols(here)]
    gin[here] = g[:, cols(here)]

    def diagonal(b):
        at = aligned(b, BLOCK)
        scores = lax.dot_general(
            cc[at], bb[at], (((1,), (1,)), ((), ())), preferred_element_type=f32
        )
        causal = iota((BLOCK, BLOCK), 0) >= iota((BLOCK, BLOCK), 1)
        cols_b, cum_b, dt_b = cols_t[at], cums[b], dts[b]
        per = 128 // hdim
        for first_head in range(0, heads, per):
            lanes = slice(first_head * hdim, (first_head + per) * hdim)
            xa_b = xa[at, lanes]
            lane = iota((BLOCK, 128), 1) // hdim
            total = jnp.zeros((BLOCK, 128), f32)
            for i in range(per):
                h = first_head + i
                seg = jnp.where(causal, cols_b[:, h : h + 1] - cum_b[h : h + 1], -jnp.inf)
                mixw = (scores * jnp.exp(seg) * dt_b[h : h + 1]).astype(bf16)
                product = jnp.dot(mixw, xa_b, preferred_element_type=f32)
                total = jnp.where(lane == i, product, total)
            yd[at, lanes] = total

    diagonal(0)

    def step(k, carry):
        state, decay = carry

        @pl.when(k != here)
        def _():
            in_g(k).wait_recv()
            in_s(k).wait_recv()

        pre[k] = state
        dec[k] = decay
        factor = gin[k]
        return state * factor + sin[k].astype(f32), decay * factor

    state, decay = lax.fori_loop(
        0, line, step, (jnp.zeros((high, wide), f32), jnp.ones((1, wide), f32))
    )
    xt[mine] = state
    xd[mine] = decay

    def line_copies(q, slot):
        device = q * line + here
        return (
            remote(xt.at[slot], xt.at[slot], xt_sem.at[0, q], xt_sem.at[1, slot], tm=device),
            remote(xd.at[slot], xd.at[slot], xd_sem.at[0, q], xd_sem.at[1, slot], tm=device),
        )

    for o in range(1, lines):
        for copy in line_copies(other_line(o), mine):
            copy.start()
    loads[2].wait()
    z[...] = jax.nn.silu(
        jnp.dot(nrm[RIM:], w_z[...], preferred_element_type=f32).astype(bf16).astype(f32)
    )
    for o in range(1, lines):
        for copy in line_copies(other_line(o), other_line(o)):
            copy.wait_recv()
    start = jnp.zeros((high, wide), f32)
    for k in range(lines):
        start = jnp.where(k < mine, start * xd[k] + xt[k], start)

    def final(k, carry):
        back[k] = (start * dec[k] + pre[k]).astype(back.dtype)
        return carry

    lax.fori_loop(0, line, final, 0)

    def out_b(q):
        return remote(
            back.at[q], hin.at[rows(here), cols(here)], b_sem.at[0, q], b_sem.at[1, here], tm=base + q
        )

    def in_b(q):
        return remote(
            back.at[q], hin.at[rows(q), cols(q)], b_sem.at[0, q], b_sem.at[1, q], tm=base + q
        )

    @pl.loop(0, line - 1)
    def _(i):
        out_b(far_first(i)).start()

    hin[rows(here), cols(here)] = back[here]
    for b in range(1, blocks):
        diagonal(b)

    @pl.loop(1, line)
    def _(o):
        in_b(other(o)).wait_recv()

    incoming = hin[...].astype(f32)
    for b in range(blocks):
        hb[b] = incoming.astype(bf16)
        incoming = incoming * totals[b] + states[b]

    share = steps // devices
    half = share // 2
    inner = channels * devices
    hit = iota((heads, channels), 0) == iota((heads, channels), 1) // hdim
    skip = jnp.sum(jnp.where(hit, column(d_skip[...]), 0.0), axis=0, keepdims=True)

    def product(k):
        at = aligned(k, share)
        yoff = jnp.dot(cc[at], hb[k * share // BLOCK], preferred_element_type=f32)
        y = yd[at] + yoff * ec[at] + skip * xa[at].astype(f32)
        gated = y * z[at]
        square = jnp.sum(gated * gated, axis=1, keepdims=True)
        sq[k] = jnp.broadcast_to(square, (share, share)).T[:1]
        scaled = (gated * norm_gain[...]).astype(bf16)
        part[at] = jnp.dot(scaled, w_out[...], preferred_element_type=f32).astype(bf16)

    def halves(k):
        begin = pl.multiple_of(k * share, share)
        return pl.ds(begin, half), pl.ds(pl.multiple_of(begin + half, half), half)

    top, bottom = pl.ds(0, half), pl.ds(half, half)
    right_top, right_bottom = halves(right)
    left_top, left_bottom = halves(left)
    across_top, across_bottom = halves(across)

    def go(n, src, dst, to):
        return remote(src, dst, send.at[n], recv.at[n], head=to)

    one = [
        go(0, part.at[across_top], first.at[0], right),
        go(1, part.at[across_bottom], first.at[1], left),
        go(2, part.at[right_bottom], full.at[0, bottom], right),
        go(3, part.at[left_top], full.at[1, top], left),
    ]

    def sq_copy(to, slot):
        return remote(sq.at[to], sqs.at[slot], sq_sem.at[0, to], sq_sem.at[1, slot], head=to)

    loads[3].wait()
    product(across)
    product(right)
    one[0].start()
    one[1].start()
    product(left)
    one[2].start()
    product(me)
    one[3].start()
    for to in (right, left, across):
        sq_copy(to, me).start()
    sqs[me] = sq[me]
    two = [
        go(4, stage.at[0], full.at[0, top], right),
        go(5, stage.at[1], full.at[1, bottom], left),
    ]
    for n, at in ((0, right_top), (1, left_bottom)):
        one[n].wait_recv()
        stage[n] = (part[at].astype(f32) + first[n].astype(f32)).astype(stage.dtype)
        two[n].start()
    for frm in (right, left, across):
        sq_copy(frm, frm).wait_recv()
    square = sqs[0]
    for k in range(1, devices):
        square = square + sqs[k]
    scale = lax.rsqrt(jnp.broadcast_to(square, (share, share)).T / inner + 1e-05)
    for copy in one[2:] + two:
        copy.wait_recv()
    own = aligned(me, share)
    own_rim = pl.ds(pl.multiple_of(me * share + RIM, RIM), share)
    for k in range(whole.shape[1] // share):
        at = pl.ds(k * share, share)
        total = part[own, at].astype(f32)
        total = total + full[0, :, at].astype(f32) + full[1, :, at].astype(f32)
        u = whole[own_rim, at].astype(f32) + emb[:, at]
        hid[own, at] = (u + scale * total).astype(hid.dtype)
    own_top, own_bottom = halves(me)
    three = [
        go(6, hid.at[own_top], hid.at[own_top], right),
        go(7, hid.at[own_bottom], hid.at[own_bottom], left),
        go(8, hid.at[own_bottom], hid.at[own_bottom], right),
        go(9, hid.at[own_top], hid.at[own_top], left),
    ]
    for copy in three:
        copy.start()
    four = [
        go(10, hid.at[left_top], hid.at[left_top], right),
        go(11, hid.at[right_bottom], hid.at[right_bottom], left),
    ]
    mix_cols = aligned(me, w_mix.shape[1])

    def finish(k):
        at = aligned(k, share)
        mixed = jnp.dot(hid[at], w_mix[...], preferred_element_type=f32)
        out[at] = hid[at, mix_cols].astype(f32) + mixed

    for copy, following in zip(three[:2], four):
        copy.wait_recv()
        following.start()
    loads[4].wait()
    finish(me)
    for copy in three[2:]:
        copy.wait_recv()
    finish(left)
    finish(right)
    for copy in four:
        copy.wait_recv()
    finish(across)
    for copy in one + two + three + four:
        copy.wait_send()
    for to in (right, left, across):
        sq_copy(to, me).wait_send()
    for o in range(1, lines):
        for copy in line_copies(other_line(o), mine):
            copy.wait_send()

    @pl.loop(1, line)
    def _(o):
        q = other(o)
        out_g(q).wait_send()
        out_s(q).wait_send()
        out_b(q).wait_send()


def layer(tms, devices, whole, emb, in_gain, w_x, w_z, w_bc, w_dt, *rest):
    f32, bf16 = jnp.float32, jnp.bfloat16
    w_mix = rest[-1]
    rows, features = whole.shape
    steps, channels, state_n = rows - RIM, w_x.shape[1], w_bc.shape[1] // 2
    heads = w_dt.shape[0]
    blocks = steps // BLOCK
    share = steps // devices
    line = min(LINE, tms)
    lines = tms // line
    high, wide = 16, 128
    while (state_n // high) * (channels // wide) > line:
        if wide < channels:
            wide *= 2
        else:
            high *= 2
    weights = (w_x, w_z, w_bc, rest[-2], w_mix)
    scratch = [(w.shape, w.dtype) for w in weights] + [
        ((rows, features), bf16),
        ((rows, channels), f32),
        ((rows, 2 * state_n), f32),
        ((steps, channels), bf16),
        ((steps, state_n), bf16),
        ((steps, state_n), bf16),
        ((blocks, heads, BLOCK), f32),
        ((blocks, heads, BLOCK), f32),
        ((steps, 128), f32),
        ((steps, channels), f32),
        ((blocks, state_n, channels), f32),
        ((blocks, 1, channels), f32),
        ((state_n, channels), bf16),
        ((1, channels), f32),
        ((steps, channels), f32),
        ((steps, channels), f32),
        ((state_n, channels), bf16),
        ((blocks, state_n, channels), bf16),
        ((steps, features), bf16),
        ((devices, 1, share), f32),
        ((line, high, wide), bf16),
        ((line, 1, wide), f32),
        ((line, high, wide), f32),
        ((line, 1, wide), f32),
        ((line, high, wide), bf16),
        ((lines, high, wide), f32),
        ((lines, 1, wide), f32),
        ((steps, features), bf16),
        ((2, share // 2, features), bf16),
        ((2, share, features), bf16),
        ((2, share // 2, features), bf16),
        ((devices, 1, share), f32),
    ]
    args = (whole, emb, in_gain, w_x, w_z, w_bc, w_dt) + rest
    return pl.pallas_call(
        functools.partial(layer_kernel, tms, line, (high, wide), devices),
        out_shape=jax.ShapeDtypeStruct((steps, w_mix.shape[1]), f32),
        in_specs=[FAR if any(a is w for w in weights) else VMEM for a in args],
        out_specs=VMEM,
        scratch_shapes=[pltpu.VMEM(shape, kind) for shape, kind in scratch]
        + [
            DMA((2, line)),
            DMA((2, line)),
            DMA((2, lines)),
            DMA((2, lines)),
            DMA((2, line)),
            DMA((12,)),
            DMA((12,)),
            DMA((2, devices)),
            DMA((len(weights),)),
        ],
        compiler_params=pltpu.CompilerParams(collective_id=1, has_side_effects=True),
        name="layer",
    )(*args)


def sinusoid(timestep, width):
    half = width // 2
    freq = jnp.exp(-math.log(10000.0) * jnp.arange(half, dtype=jnp.float32) / half)
    angle = timestep.astype(jnp.float32)[0] * freq
    return jnp.concatenate([jnp.sin(angle), jnp.cos(angle)])


def shards(
    latent,
    timestep,
    in_gain,
    w_x,
    w_z,
    w_bc,
    w_dt,
    conv_x,
    conv_bc,
    dt_bias,
    a_log,
    d_skip,
    norm_gain,
    w_out,
    w_mix,
):
    tms, devices = lax.axis_size("tm"), lax.axis_size("head")
    whole = gather(latent, tms, devices)
    return layer(
        tms,
        devices,
        whole,
        sinusoid(timestep, whole.shape[1])[None, :],
        in_gain[None, :],
        w_x,
        w_z,
        w_bc,
        w_dt.T,
        conv_x,
        conv_bc,
        dt_bias[None, :],
        a_log[None, :],
        d_skip[None, :],
        norm_gain[None, :],
        w_out,
        w_mix,
    ).astype(jnp.bfloat16)


def solution(mesh):
    in_specs = (
        P("tm", "head"),
        P(),
        P(),
        P(None, "head"),
        P(None, "head"),
        P(),
        P(None, "head"),
        P(None, "head"),
        P(),
        P("head"),
        P("head"),
        P("head"),
        P("head"),
        P("head", None),
        P(None, "head"),
    )
    out_specs = P("tm", "head")
    return jax.shard_map(shards, mesh=mesh, in_specs=in_specs, out_specs=out_specs, check_vma=False)
```

```python
import functools
import math

import jax
import jax.numpy as jnp
from jax import lax
from jax.experimental import pallas as pl
from jax.experimental.pallas import tpu as pltpu
from jax.sharding import PartitionSpec as P

BLOCK = 256
RIM = 16
LINE = 32
MESH = pl.DeviceIdType.MESH
VMEM = pl.BlockSpec(memory_space=pltpu.VMEM)
FAR = pl.BlockSpec(memory_space=pl.ANY)
DMA = pltpu.SemaphoreType.DMA


def remote(src, dst, send, recv, **device):
    return pltpu.make_async_remote_copy(
        src_ref=src, dst_ref=dst, send_sem=send, recv_sem=recv, device_id=device, device_id_type=MESH
    )


def greet(devices, count):
    barrier = pltpu.get_barrier_semaphore()
    for device in devices:
        pl.semaphore_signal(barrier, inc=1, device_id=device, device_id_type=MESH)
    pl.semaphore_wait(barrier, count)


def aligned(index, size):
    return pl.ds(pl.multiple_of(index * size, size), size)


def gather_kernel(tms, heads, lat, out, own_sem, send, recv, rim_send, rim_recv):
    tm, me = lax.axis_index("tm"), lax.axis_index("head")
    right, left = lax.rem(me + 1, heads), lax.rem(me + heads - 1, heads)
    later, earlier = lax.rem(tm + 1, tms), lax.rem(tm + tms - 1, tms)
    rows, width = lat.shape
    half = rows // 2
    greet(
        [{"head": left}, {"head": right}] + [{"tm": earlier, "head": h} for h in range(heads)],
        2 + heads,
    )
    top, bottom = pl.ds(RIM, half), pl.ds(RIM + half, half)
    mine, lefts, rights = aligned(me, width), aligned(left, width), aligned(right, width)

    def own(rows_out, start, sem, to):
        return remote(
            lat.at[pl.ds(start, half)], out.at[rows_out, mine], send.at[sem], recv.at[sem], head=to
        )

    copies = [
        own(top, 0, 0, right),
        own(bottom, half, 1, left),
        own(bottom, half, 2, right),
        own(top, 0, 3, left),
    ]
    for copy in copies[:2]:
        copy.start()
    rims = [
        remote(
            lat.at[pl.ds(rows - RIM, RIM)],
            out.at[pl.ds(0, RIM), mine],
            rim_send.at[h],
            rim_recv.at[me],
            tm=later,
            head=h,
        )
        for h in range(heads)
    ]
    for copy in rims:
        copy.start()
    for copy in copies[2:]:
        copy.start()
    keep = pltpu.make_async_copy(lat, out.at[pl.ds(RIM, rows), mine], own_sem)
    keep.start()
    onward = [
        remote(out.at[top, lefts], out.at[top, lefts], send.at[4], recv.at[4], head=right),
        remote(out.at[bottom, rights], out.at[bottom, rights], send.at[5], recv.at[5], head=left),
    ]
    for copy, following in zip(copies[:2], onward):
        copy.wait_recv()
        following.start()
    for copy in copies[2:] + onward:
        copy.wait_recv()
    for h in range(heads):
        remote(
            lat.at[pl.ds(rows - RIM, RIM)],
            out.at[pl.ds(0, RIM), pl.ds(h * width, width)],
            rim_send.at[h],
            rim_recv.at[h],
            tm=later,
            head=h,
        ).wait_recv()
    for copy in copies + onward + rims:
        copy.wait_send()
    keep.wait()


def gather(lat, tms, heads):
    rows, width = lat.shape
    return pl.pallas_call(
        functools.partial(gather_kernel, tms, heads),
        out_shape=jax.ShapeDtypeStruct((rows + RIM, width * heads), lat.dtype),
        in_specs=[VMEM],
        out_specs=VMEM,
        scratch_shapes=[DMA, DMA((6,)), DMA((6,)), DMA((heads,)), DMA((heads,))],
        compiler_params=pltpu.CompilerParams(collective_id=0, has_side_effects=True),
        name="gather_rows",
    )(lat)


def split(value):
    parts = []
    for _ in range(3):
        part = value.astype(jnp.bfloat16)
        parts.append(part)
        value = value - part.astype(jnp.float32)
    return parts


def exact(value, ones):
    total = None
    for part in split(value):
        term = jnp.dot(part, ones, preferred_element_type=jnp.float32)
        total = term if total is None else total + term
    return total


def iota(shape, axis):
    return lax.broadcasted_iota(jnp.int32, shape, axis)


def column(row):
    count = row.shape[1]
    wide = jnp.broadcast_to(row, (count, count))
    return jnp.sum(
        jnp.where(iota((count, count), 0) == iota((count, count), 1), wide, 0.0), axis=1, keepdims=True
    )


def layer_kernel(
    tms,
    line,
    piece,
    devices,
    whole,
    emb,
    in_gain,
    w_x_far,
    w_z_far,
    w_bc_far,
    w_dt,
    conv_x,
    conv_bc,
    dt_bias,
    a_log,
    d_skip,
    norm_gain,
    w_out_far,
    w_mix_far,
    out,
    w_x,
    w_z,
    w_bc,
    w_out,
    w_mix,
    nrm,
    xs,
    bcs,
    xa,
    bb,
    cc,
    cums,
    dts,
    cols_t,
    ec,
    states,
    totals,
    s,
    g,
    yd,
    z,
    hin,
    hb,
    part,
    sq,
    sin,
    gin,
    pre,
    dec,
    back,
    xt,
    xd,
    hid,
    first,
    full,
    stage,
    sqs,
    s_sem,
    g_sem,
    xt_sem,
    xd_sem,
    b_sem,
    send,
    recv,
    sq_sem,
    w_sem,
):
    f32, bf16 = jnp.float32, jnp.bfloat16
    lines = tms // line
    tm = lax.axis_index("tm")
    here, mine = lax.rem(tm, line), tm // line
    base = mine * line
    high, wide = piece
    stack = s.shape[0] // high
    me = lax.axis_index("head")
    right, left, across = (lax.rem(me + d, devices) for d in (1, devices - 1, 2))

    def rows(k):
        return aligned(lax.rem(k, stack), high)

    def cols(k):
        return aligned(k // stack, wide)

    def other(o):
        return lax.rem(here + o, line)

    def other_line(o):
        return lax.rem(mine + o, lines)

    def far_first(i):
        away = (i + 1) // 2
        return other(line // 2 + jnp.where(lax.rem(i, 2) == 0, away, -away))

    pairs = ((w_x_far, w_x), (w_bc_far, w_bc), (w_z_far, w_z), (w_out_far, w_out), (w_mix_far, w_mix))
    loads = [pltpu.make_async_copy(far, near, w_sem.at[n]) for n, (far, near) in enumerate(pairs)]
    for load in loads:
        load.start()
    barrier = pltpu.get_barrier_semaphore()

    @pl.loop(0, line - 1)
    def _(i):
        pl.semaphore_signal(barrier, inc=1, device_id={"tm": base + far_first(i)}, device_id_type=MESH)

    for o in range(1, lines):
        pl.semaphore_signal(
            barrier, inc=1, device_id={"tm": other_line(o) * line + here}, device_id_type=MESH
        )
    for device in (left, right, across):
        pl.semaphore_signal(barrier, inc=1, device_id={"head": device}, device_id_type=MESH)

    total_rows = whole.shape[0]
    steps = total_rows - RIM
    chunk = total_rows // 11

    @pl.loop(0, 11)
    def _(c):
        at = aligned(c, chunk)
        u = whole[at].astype(f32) + emb[...]
        mean = jnp.mean(u * u, axis=1, keepdims=True)
        nrm[at] = (u * lax.rsqrt(mean + 1e-05) * in_gain[...]).astype(bf16)

    dt_t = lax.dot_general(
        w_dt[...], nrm[RIM:], (((1,), (1,)), ((), ())), preferred_element_type=f32
    )
    loads[0].wait()
    xs[...] = jnp.dot(nrm[...], w_x[...], preferred_element_type=f32).astype(bf16).astype(f32)
    loads[1].wait()
    bcs[...] = jnp.dot(nrm[...], w_bc[...], preferred_element_type=f32).astype(bf16).astype(f32)

    @pl.when(tm == 0)
    def _():
        xs[:RIM] = jnp.zeros((RIM, xs.shape[1]), f32)
        bcs[:RIM] = jnp.zeros((RIM, bcs.shape[1]), f32)

    taps = conv_x.shape[0]
    state_n = bb.shape[1]
    width = 128

    def conv(source, kernel, c, lanes):
        value = source[pl.ds(pl.multiple_of(c * width + RIM - 8, 8), width + 8), lanes]
        total = jnp.zeros((width, value.shape[1]), f32)
        for k in range(taps):
            at = 8 - taps + 1 + k
            total = total + value[at : at + width] * kernel[k : k + 1, lanes]
        return jax.nn.silu(total).astype(bf16)

    @pl.loop(0, steps // width)
    def _(c):
        at = aligned(c, width)
        for lane in range(0, xs.shape[1], 128):
            lanes = pl.ds(lane, 128)
            xa[at, lanes] = conv(xs, conv_x, c, lanes)
        bb[at] = conv(bcs, conv_bc, c, pl.ds(0, state_n))
        cc[at] = conv(bcs, conv_bc, c, pl.ds(state_n, state_n))

    raw = dt_t + column(dt_bias[...])
    dt_t = jnp.maximum(raw, 0.0) + jnp.log1p(jnp.exp(-jnp.abs(raw)))
    la_t = dt_t * -jnp.exp(column(a_log[...]))
    heads = dt_t.shape[0]
    channels = xa.shape[1]
    hdim = channels // heads
    blocks = steps // BLOCK
    upper = jnp.where(iota((BLOCK, BLOCK), 0) <= iota((BLOCK, BLOCK), 1), 1.0, 0.0).astype(bf16)

    def picks(offset):
        hit = iota((128, channels), 0) == iota((128, channels), 1) // hdim + offset
        return jnp.where(hit, 1.0, 0.0).astype(bf16)

    tail_picks, decay_picks = picks(heads), picks(2 * heads)
    for b in range(blocks):
        span = slice(b * BLOCK, (b + 1) * BLOCK)
        dt_b = dt_t[:, span]
        cum_b = exact(la_t[:, span], upper)
        last = cum_b[:, BLOCK - 1 :]
        tail = jnp.exp(last - cum_b) * dt_b
        cums[b] = cum_b
        dts[b] = dt_b
        pad = jnp.zeros((128 - 3 * heads, BLOCK), f32)
        columns = jnp.concatenate([cum_b, tail, jnp.exp(cum_b), pad], axis=0).T
        cols_t[span] = columns
        ec[span] = exact(columns, decay_picks)
        weighted = (xa[span].astype(f32) * exact(columns, tail_picks)).astype(bf16)
        states[b] = jnp.dot(
            bb[span].astype(f32).T.astype(bf16), weighted, preferred_element_type=f32
        )
        totals[b] = ec[(b + 1) * BLOCK - 1 : (b + 1) * BLOCK]
    run_state, run_total = states[0], totals[0]
    for b in range(1, blocks):
        run_state, run_total = run_state * totals[b] + states[b], run_total * totals[b]
    s[...] = run_state.astype(bf16)
    g[...] = run_total
    pl.semaphore_wait(barrier, line - 1 + lines - 1 + 3)

    def out_s(q):
        return remote(s.at[rows(q), cols(q)], sin.at[here], s_sem.at[0, q], s_sem.at[1, here], tm=base + q)

    def out_g(q):
        return remote(g.at[:, cols(q)], gin.at[here], g_sem.at[0, q], g_sem.at[1, here], tm=base + q)

    def in_s(q):
        return remote(s.at[rows(q), cols(q)], sin.at[q], s_sem.at[0, q], s_sem.at[1, q], tm=base + q)

    def in_g(q):
        return remote(g.at[:, cols(q)], gin.at[q], g_sem.at[0, q], g_sem.at[1, q], tm=base + q)

    @pl.loop(0, line - 1)
    def _(i):
        q = far_first(i)
        out_g(q).start()
        out_s(q).start()

    sin[here] = s[rows(here), cols(here)]
    gin[here] = g[:, cols(here)]

    def diagonal(b):
        at = aligned(b, BLOCK)
        scores = lax.dot_general(
            cc[at], bb[at], (((1,), (1,)), ((), ())), preferred_element_type=f32
        )
        causal = iota((BLOCK, BLOCK), 0) >= iota((BLOCK, BLOCK), 1)
        cols_b, cum_b, dt_b = cols_t[at], cums[b], dts[b]
        per = 128 // hdim
        for first_head in range(0, heads, per):
            lanes = slice(first_head * hdim, (first_head + per) * hdim)
            xa_b = xa[at, lanes]
            lane = iota((BLOCK, 128), 1) // hdim
            total = jnp.zeros((BLOCK, 128), f32)
            for i in range(per):
                h = first_head + i
                seg = jnp.where(causal, cols_b[:, h : h + 1] - cum_b[h : h + 1], -jnp.inf)
                mixw = (scores * jnp.exp(seg) * dt_b[h : h + 1]).astype(bf16)
                product = jnp.dot(mixw, xa_b, preferred_element_type=f32)
                total = jnp.where(lane == i, product, total)
            yd[at, lanes] = total

    diagonal(0)

    def step(k, carry):
        state, decay = carry

        @pl.when(k != here)
        def _():
            in_g(k).wait_recv()
            in_s(k).wait_recv()

        pre[k] = state
        dec[k] = decay
        factor = gin[k]
        return state * factor + sin[k].astype(f32), decay * factor

    state, decay = lax.fori_loop(
        0, line, step, (jnp.zeros((high, wide), f32), jnp.ones((1, wide), f32))
    )
    xt[mine] = state
    xd[mine] = decay

    def line_copies(q, slot):
        device = q * line + here
        return (
            remote(xt.at[slot], xt.at[slot], xt_sem.at[0, q], xt_sem.at[1, slot], tm=device),
            remote(xd.at[slot], xd.at[slot], xd_sem.at[0, q], xd_sem.at[1, slot], tm=device),
        )

    for o in range(1, lines):
        for copy in line_copies(other_line(o), mine):
            copy.start()
    loads[2].wait()
    z[...] = jax.nn.silu(
        jnp.dot(nrm[RIM:], w_z[...], preferred_element_type=f32).astype(bf16).astype(f32)
    )
    for o in range(1, lines):
        for copy in line_copies(other_line(o), other_line(o)):
            copy.wait_recv()
    start = jnp.zeros((high, wide), f32)
    for k in range(lines):
        start = jnp.where(k < mine, start * xd[k] + xt[k], start)

    def final(k, carry):
        back[k] = (start * dec[k] + pre[k]).astype(back.dtype)
        return carry

    lax.fori_loop(0, line, final, 0)

    def out_b(q):
        return remote(
            back.at[q], hin.at[rows(here), cols(here)], b_sem.at[0, q], b_sem.at[1, here], tm=base + q
        )

    def in_b(q):
        return remote(
            back.at[q], hin.at[rows(q), cols(q)], b_sem.at[0, q], b_sem.at[1, q], tm=base + q
        )

    @pl.loop(0, line - 1)
    def _(i):
        out_b(far_first(i)).start()

    hin[rows(here), cols(here)] = back[here]
    for b in range(1, blocks):
        diagonal(b)

    @pl.loop(1, line)
    def _(o):
        in_b(other(o)).wait_recv()

    incoming = hin[...].astype(f32)
    for b in range(blocks):
        hb[b] = incoming.astype(bf16)
        incoming = incoming * totals[b] + states[b]

    share = steps // devices
    half = share // 2
    inner = channels * devices
    hit = iota((heads, channels), 0) == iota((heads, channels), 1) // hdim
    skip = jnp.sum(jnp.where(hit, column(d_skip[...]), 0.0), axis=0, keepdims=True)

    def product(k):
        at = aligned(k, share)
        yoff = jnp.dot(cc[at], hb[k * share // BLOCK], preferred_element_type=f32)
        y = yd[at] + yoff * ec[at] + skip * xa[at].astype(f32)
        gated = y * z[at]
        square = jnp.sum(gated * gated, axis=1, keepdims=True)
        sq[k] = jnp.broadcast_to(square, (share, share)).T[:1]
        scaled = (gated * norm_gain[...]).astype(bf16)
        part[at] = jnp.dot(scaled, w_out[...], preferred_element_type=f32).astype(bf16)

    features = whole.shape[1]
    low, up = pl.ds(0, features // 2), pl.ds(features // 2, features // 2)

    def half_of(k, n):
        return pl.ds(pl.multiple_of(k * share + n * half, half), half)

    def go(n, src, dst, to):
        return remote(src, dst, send.at[n], recv.at[n], head=to)

    def sums(n):
        at = pl.ds(n * half, half)
        base_sem = 12 * n
        return (
            [
                go(base_sem, part.at[half_of(across, n), low], first.at[0, at], right),
                go(base_sem + 1, part.at[half_of(across, n), up], first.at[1, at], left),
                go(base_sem + 2, part.at[half_of(right, n), up], full.at[0, at, up], right),
                go(base_sem + 3, part.at[half_of(left, n), low], full.at[1, at, low], left),
            ],
            [
                go(base_sem + 4, stage.at[0, at], full.at[0, at, low], right),
                go(base_sem + 5, stage.at[1, at], full.at[1, at, up], left),
            ],
        )

    def hides(n):
        own, lefts, rights = half_of(me, n), half_of(left, n), half_of(right, n)
        base_sem = 12 * n
        return (
            [
                go(base_sem + 6, hid.at[own, low], hid.at[own, low], right),
                go(base_sem + 7, hid.at[own, up], hid.at[own, up], left),
                go(base_sem + 8, hid.at[own, up], hid.at[own, up], right),
                go(base_sem + 9, hid.at[own, low], hid.at[own, low], left),
            ],
            [
                go(base_sem + 10, hid.at[lefts, low], hid.at[lefts, low], right),
                go(base_sem + 11, hid.at[rights, up], hid.at[rights, up], left),
            ],
        )

    def sq_copy(to, slot):
        return remote(sq.at[to], sqs.at[slot], sq_sem.at[0, to], sq_sem.at[1, slot], head=to)

    ones, twos = zip(*[sums(n) for n in range(2)])
    threes, fours = zip(*[hides(n) for n in range(2)])
    loads[3].wait()
    product(across)
    product(right)
    ones[0][0].start()
    ones[0][1].start()
    product(left)
    ones[0][2].start()
    ones[0][3].start()
    product(me)
    for to in (right, left, across):
        sq_copy(to, me).start()
    for copy in ones[1][:2]:
        copy.start()
    sqs[me] = sq[me]

    def pass_on(n):
        at = pl.ds(n * half, half)
        for d, k, lanes in ((0, right, low), (1, left, up)):
            ones[n][d].wait_recv()
            value = part[half_of(k, n), lanes].astype(f32) + first[d, at].astype(f32)
            stage[d, at] = value.astype(stage.dtype)
            twos[n][d].start()

    pass_on(0)
    for copy in ones[1][2:]:
        copy.start()
    pass_on(1)
    for frm in (right, left, across):
        sq_copy(frm, frm).wait_recv()
    square = sqs[0]
    for k in range(1, devices):
        square = square + sqs[k]
    scale = lax.rsqrt(jnp.broadcast_to(square, (share, share)).T / inner + 1e-05)
    for n in range(2):
        for copy in ones[n][2:] + twos[n]:
            copy.wait_recv()
        at, own = pl.ds(n * half, half), half_of(me, n)
        own_rim = pl.ds(pl.multiple_of(me * share + n * half + RIM, RIM), half)
        for k in range(features // share):
            lanes = pl.ds(k * share, share)
            total = part[own, lanes].astype(f32)
            total = total + full[0, at, lanes].astype(f32) + full[1, at, lanes].astype(f32)
            u = whole[own_rim, lanes].astype(f32) + emb[:, lanes]
            hid[own, lanes] = (u + scale[n * half : (n + 1) * half] * total).astype(hid.dtype)
        for copy in threes[n]:
            copy.start()
    mix_cols = aligned(me, w_mix.shape[1])

    def finish(at):
        mixed = jnp.dot(hid[at], w_mix[...], preferred_element_type=f32)
        out[at] = hid[at, mix_cols].astype(f32) + mixed

    for n in range(2):
        for copy, following in zip(threes[n][:2], fours[n]):
            copy.wait_recv()
            following.start()
        if n == 0:
            loads[4].wait()
            finish(aligned(me, share))
    for n in range(2):
        for copy in threes[n][2:]:
            copy.wait_recv()
    finish(aligned(left, share))
    finish(aligned(right, share))
    for n in range(2):
        for copy in fours[n]:
            copy.wait_recv()
        finish(half_of(across, n))
    for n in range(2):
        for copy in ones[n] + twos[n] + threes[n] + fours[n]:
            copy.wait_send()
    for to in (right, left, across):
        sq_copy(to, me).wait_send()
    for o in range(1, lines):
        for copy in line_copies(other_line(o), mine):
            copy.wait_send()

    @pl.loop(1, line)
    def _(o):
        q = other(o)
        out_g(q).wait_send()
        out_s(q).wait_send()
        out_b(q).wait_send()


def layer(tms, devices, whole, emb, in_gain, w_x, w_z, w_bc, w_dt, *rest):
    f32, bf16 = jnp.float32, jnp.bfloat16
    w_mix = rest[-1]
    rows, features = whole.shape
    steps, channels, state_n = rows - RIM, w_x.shape[1], w_bc.shape[1] // 2
    heads = w_dt.shape[0]
    blocks = steps // BLOCK
    share = steps // devices
    line = min(LINE, tms)
    lines = tms // line
    high, wide = 16, 128
    while (state_n // high) * (channels // wide) > line:
        if wide < channels:
            wide *= 2
        else:
            high *= 2
    weights = (w_x, w_z, w_bc, rest[-2], w_mix)
    scratch = [(w.shape, w.dtype) for w in weights] + [
        ((rows, features), bf16),
        ((rows, channels), f32),
        ((rows, 2 * state_n), f32),
        ((steps, channels), bf16),
        ((steps, state_n), bf16),
        ((steps, state_n), bf16),
        ((blocks, heads, BLOCK), f32),
        ((blocks, heads, BLOCK), f32),
        ((steps, 128), f32),
        ((steps, channels), f32),
        ((blocks, state_n, channels), f32),
        ((blocks, 1, channels), f32),
        ((state_n, channels), bf16),
        ((1, channels), f32),
        ((steps, channels), f32),
        ((steps, channels), f32),
        ((state_n, channels), bf16),
        ((blocks, state_n, channels), bf16),
        ((steps, features), bf16),
        ((devices, 1, share), f32),
        ((line, high, wide), bf16),
        ((line, 1, wide), f32),
        ((line, high, wide), f32),
        ((line, 1, wide), f32),
        ((line, high, wide), bf16),
        ((lines, high, wide), f32),
        ((lines, 1, wide), f32),
        ((steps, features), bf16),
        ((2, share, features // 2), bf16),
        ((2, share, features), bf16),
        ((2, share, features // 2), bf16),
        ((devices, 1, share), f32),
    ]
    args = (whole, emb, in_gain, w_x, w_z, w_bc, w_dt) + rest
    return pl.pallas_call(
        functools.partial(layer_kernel, tms, line, (high, wide), devices),
        out_shape=jax.ShapeDtypeStruct((steps, w_mix.shape[1]), f32),
        in_specs=[FAR if any(a is w for w in weights) else VMEM for a in args],
        out_specs=VMEM,
        scratch_shapes=[pltpu.VMEM(shape, kind) for shape, kind in scratch]
        + [
            DMA((2, line)),
            DMA((2, line)),
            DMA((2, lines)),
            DMA((2, lines)),
            DMA((2, line)),
            DMA((24,)),
            DMA((24,)),
            DMA((2, devices)),
            DMA((len(weights),)),
        ],
        compiler_params=pltpu.CompilerParams(collective_id=1, has_side_effects=True),
        name="layer",
    )(*args)


def sinusoid(timestep, width):
    half = width // 2
    freq = jnp.exp(-math.log(10000.0) * jnp.arange(half, dtype=jnp.float32) / half)
    angle = timestep.astype(jnp.float32)[0] * freq
    return jnp.concatenate([jnp.sin(angle), jnp.cos(angle)])


def shards(
    latent,
    timestep,
    in_gain,
    w_x,
    w_z,
    w_bc,
    w_dt,
    conv_x,
    conv_bc,
    dt_bias,
    a_log,
    d_skip,
    norm_gain,
    w_out,
    w_mix,
):
    tms, devices = lax.axis_size("tm"), lax.axis_size("head")
    whole = gather(latent, tms, devices)
    return layer(
        tms,
        devices,
        whole,
        sinusoid(timestep, whole.shape[1])[None, :],
        in_gain[None, :],
        w_x,
        w_z,
        w_bc,
        w_dt.T,
        conv_x,
        conv_bc,
        dt_bias[None, :],
        a_log[None, :],
        d_skip[None, :],
        norm_gain[None, :],
        w_out,
        w_mix,
    ).astype(jnp.bfloat16)


def solution(mesh):
    in_specs = (
        P("tm", "head"),
        P(),
        P(),
        P(None, "head"),
        P(None, "head"),
        P(),
        P(None, "head"),
        P(None, "head"),
        P(),
        P("head"),
        P("head"),
        P("head"),
        P("head"),
        P("head", None),
        P(None, "head"),
    )
    out_specs = P("tm", "head")
    return jax.shard_map(shards, mesh=mesh, in_specs=in_specs, out_specs=out_specs, check_vma=False)
```

```python
import functools
import math

import jax
import jax.numpy as jnp
from jax import lax
from jax.experimental import pallas as pl
from jax.experimental.pallas import tpu as pltpu
from jax.sharding import PartitionSpec as P

BLOCK = 256
RIM = 16
LINE = 32
MESH = pl.DeviceIdType.MESH
VMEM = pl.BlockSpec(memory_space=pltpu.VMEM)
FAR = pl.BlockSpec(memory_space=pl.ANY)
DMA = pltpu.SemaphoreType.DMA


def remote(src, dst, send, recv, **device):
    return pltpu.make_async_remote_copy(
        src_ref=src, dst_ref=dst, send_sem=send, recv_sem=recv, device_id=device, device_id_type=MESH
    )


def greet(devices, count):
    barrier = pltpu.get_barrier_semaphore()
    for device in devices:
        pl.semaphore_signal(barrier, inc=1, device_id=device, device_id_type=MESH)
    pl.semaphore_wait(barrier, count)


def aligned(index, size):
    return pl.ds(pl.multiple_of(index * size, size), size)


def gather_kernel(tms, heads, lat, out, own_sem, send, recv, rim_send, rim_recv):
    tm, me = lax.axis_index("tm"), lax.axis_index("head")
    right, left = lax.rem(me + 1, heads), lax.rem(me + heads - 1, heads)
    later, earlier = lax.rem(tm + 1, tms), lax.rem(tm + tms - 1, tms)
    rows, width = lat.shape
    half = rows // 2
    greet(
        [{"head": left}, {"head": right}] + [{"tm": earlier, "head": h} for h in range(heads)],
        2 + heads,
    )
    top, bottom = pl.ds(RIM, half), pl.ds(RIM + half, half)
    mine, lefts, rights = aligned(me, width), aligned(left, width), aligned(right, width)

    def own(rows_out, start, sem, to):
        return remote(
            lat.at[pl.ds(start, half)], out.at[rows_out, mine], send.at[sem], recv.at[sem], head=to
        )

    copies = [
        own(top, 0, 0, right),
        own(bottom, half, 1, left),
        own(bottom, half, 2, right),
        own(top, 0, 3, left),
    ]
    for copy in copies[:2]:
        copy.start()
    rims = [
        remote(
            lat.at[pl.ds(rows - RIM, RIM)],
            out.at[pl.ds(0, RIM), mine],
            rim_send.at[h],
            rim_recv.at[me],
            tm=later,
            head=h,
        )
        for h in range(heads)
    ]
    for copy in rims:
        copy.start()
    for copy in copies[2:]:
        copy.start()
    keep = pltpu.make_async_copy(lat, out.at[pl.ds(RIM, rows), mine], own_sem)
    keep.start()
    onward = [
        remote(out.at[top, lefts], out.at[top, lefts], send.at[4], recv.at[4], head=right),
        remote(out.at[bottom, rights], out.at[bottom, rights], send.at[5], recv.at[5], head=left),
    ]
    for copy, following in zip(copies[:2], onward):
        copy.wait_recv()
        following.start()
    for copy in copies[2:] + onward:
        copy.wait_recv()
    for h in range(heads):
        remote(
            lat.at[pl.ds(rows - RIM, RIM)],
            out.at[pl.ds(0, RIM), pl.ds(h * width, width)],
            rim_send.at[h],
            rim_recv.at[h],
            tm=later,
            head=h,
        ).wait_recv()
    for copy in copies + onward + rims:
        copy.wait_send()
    keep.wait()


def gather(lat, tms, heads):
    rows, width = lat.shape
    return pl.pallas_call(
        functools.partial(gather_kernel, tms, heads),
        out_shape=jax.ShapeDtypeStruct((rows + RIM, width * heads), lat.dtype),
        in_specs=[VMEM],
        out_specs=VMEM,
        scratch_shapes=[DMA, DMA((6,)), DMA((6,)), DMA((heads,)), DMA((heads,))],
        compiler_params=pltpu.CompilerParams(collective_id=0, has_side_effects=True),
        name="gather_rows",
    )(lat)


def split(value):
    parts = []
    for _ in range(3):
        part = value.astype(jnp.bfloat16)
        parts.append(part)
        value = value - part.astype(jnp.float32)
    return parts


def exact(value, ones):
    total = None
    for part in split(value):
        term = jnp.dot(part, ones, preferred_element_type=jnp.float32)
        total = term if total is None else total + term
    return total


def iota(shape, axis):
    return lax.broadcasted_iota(jnp.int32, shape, axis)


def column(row):
    count = row.shape[1]
    wide = jnp.broadcast_to(row, (count, count))
    return jnp.sum(
        jnp.where(iota((count, count), 0) == iota((count, count), 1), wide, 0.0), axis=1, keepdims=True
    )


def layer_kernel(
    tms,
    line,
    piece,
    devices,
    whole,
    emb,
    in_gain,
    w_x_far,
    w_z_far,
    w_bc_far,
    w_dt,
    conv_x,
    conv_bc,
    dt_bias,
    a_log,
    d_skip,
    norm_gain,
    w_out_far,
    w_mix_far,
    out,
    w_x,
    w_z,
    w_bc,
    w_out,
    w_mix,
    nrm,
    xs,
    bcs,
    xa,
    bb,
    cc,
    cums,
    dts,
    cols_t,
    ec,
    states,
    totals,
    s,
    g,
    yd,
    z,
    hin,
    hb,
    part,
    sq,
    sin,
    gin,
    pre,
    dec,
    back,
    xt,
    xd,
    hid,
    first,
    full,
    stage,
    sqs,
    pg,
    ps,
    sf,
    gf,
    gc,
    sc,
    hc,
    give,
    got,
    s_sem,
    g_sem,
    xt_sem,
    xd_sem,
    b_sem,
    send,
    recv,
    sq_sem,
    w_sem,
    pair_sem,
):
    f32, bf16 = jnp.float32, jnp.bfloat16
    lines = tms // line
    tm = lax.axis_index("tm")
    chips = line // 2
    place, mine = lax.rem(tm, line), tm // line
    here, core = place // 2, lax.rem(place, 2)
    base = mine * line + core
    partner = tm + 1 - 2 * core
    high, wide = piece
    stack = s.shape[0] // high
    me = lax.axis_index("head")
    right, left, across = (lax.rem(me + d, devices) for d in (1, devices - 1, 2))

    def rows(k):
        return aligned(lax.rem(k, stack), high)

    def cols(k):
        return aligned(k // stack, wide)

    def other(o):
        return lax.rem(here + o, chips)

    def other_line(o):
        return lax.rem(mine + o, lines)

    def far_first(i):
        away = (i + 1) // 2
        return other(chips // 2 + jnp.where(lax.rem(i, 2) == 0, away, -away))

    pairs = ((w_x_far, w_x), (w_bc_far, w_bc), (w_z_far, w_z), (w_out_far, w_out), (w_mix_far, w_mix))
    loads = [pltpu.make_async_copy(far, near, w_sem.at[n]) for n, (far, near) in enumerate(pairs)]
    for load in loads:
        load.start()
    barrier = pltpu.get_barrier_semaphore()

    @pl.loop(0, chips - 1)
    def _(i):
        pl.semaphore_signal(barrier, inc=1, device_id={"tm": base + 2 * far_first(i)}, device_id_type=MESH)

    for o in range(1, lines):
        pl.semaphore_signal(
            barrier, inc=1, device_id={"tm": other_line(o) * line + place}, device_id_type=MESH
        )
    pl.semaphore_signal(barrier, inc=1, device_id={"tm": partner}, device_id_type=MESH)
    for device in (left, right, across):
        pl.semaphore_signal(barrier, inc=1, device_id={"head": device}, device_id_type=MESH)

    total_rows = whole.shape[0]
    steps = total_rows - RIM
    chunk = total_rows // 11

    @pl.loop(0, 11)
    def _(c):
        at = aligned(c, chunk)
        u = whole[at].astype(f32) + emb[...]
        mean = jnp.mean(u * u, axis=1, keepdims=True)
        nrm[at] = (u * lax.rsqrt(mean + 1e-05) * in_gain[...]).astype(bf16)

    dt_t = lax.dot_general(
        w_dt[...], nrm[RIM:], (((1,), (1,)), ((), ())), preferred_element_type=f32
    )
    loads[0].wait()
    xs[...] = jnp.dot(nrm[...], w_x[...], preferred_element_type=f32).astype(bf16).astype(f32)
    loads[1].wait()
    bcs[...] = jnp.dot(nrm[...], w_bc[...], preferred_element_type=f32).astype(bf16).astype(f32)

    @pl.when(tm == 0)
    def _():
        xs[:RIM] = jnp.zeros((RIM, xs.shape[1]), f32)
        bcs[:RIM] = jnp.zeros((RIM, bcs.shape[1]), f32)

    taps = conv_x.shape[0]
    state_n = bb.shape[1]
    width = 128

    def conv(source, kernel, c, lanes):
        value = source[pl.ds(pl.multiple_of(c * width + RIM - 8, 8), width + 8), lanes]
        total = jnp.zeros((width, value.shape[1]), f32)
        for k in range(taps):
            at = 8 - taps + 1 + k
            total = total + value[at : at + width] * kernel[k : k + 1, lanes]
        return jax.nn.silu(total).astype(bf16)

    @pl.loop(0, steps // width)
    def _(c):
        at = aligned(c, width)
        for lane in range(0, xs.shape[1], 128):
            lanes = pl.ds(lane, 128)
            xa[at, lanes] = conv(xs, conv_x, c, lanes)
        bb[at] = conv(bcs, conv_bc, c, pl.ds(0, state_n))
        cc[at] = conv(bcs, conv_bc, c, pl.ds(state_n, state_n))

    raw = dt_t + column(dt_bias[...])
    dt_t = jnp.maximum(raw, 0.0) + jnp.log1p(jnp.exp(-jnp.abs(raw)))
    la_t = dt_t * -jnp.exp(column(a_log[...]))
    heads = dt_t.shape[0]
    channels = xa.shape[1]
    hdim = channels // heads
    blocks = steps // BLOCK
    upper = jnp.where(iota((BLOCK, BLOCK), 0) <= iota((BLOCK, BLOCK), 1), 1.0, 0.0).astype(bf16)

    def picks(offset):
        hit = iota((128, channels), 0) == iota((128, channels), 1) // hdim + offset
        return jnp.where(hit, 1.0, 0.0).astype(bf16)

    tail_picks, decay_picks = picks(heads), picks(2 * heads)
    for b in range(blocks):
        span = slice(b * BLOCK, (b + 1) * BLOCK)
        dt_b = dt_t[:, span]
        cum_b = exact(la_t[:, span], upper)
        last = cum_b[:, BLOCK - 1 :]
        tail = jnp.exp(last - cum_b) * dt_b
        cums[b] = cum_b
        dts[b] = dt_b
        pad = jnp.zeros((128 - 3 * heads, BLOCK), f32)
        columns = jnp.concatenate([cum_b, tail, jnp.exp(cum_b), pad], axis=0).T
        cols_t[span] = columns
        ec[span] = exact(columns, decay_picks)
        weighted = (xa[span].astype(f32) * exact(columns, tail_picks)).astype(bf16)
        states[b] = jnp.dot(
            bb[span].astype(f32).T.astype(bf16), weighted, preferred_element_type=f32
        )
        totals[b] = ec[(b + 1) * BLOCK - 1 : (b + 1) * BLOCK]
    run_state, run_total = states[0], totals[0]
    for b in range(1, blocks):
        run_state, run_total = run_state * totals[b] + states[b], run_total * totals[b]
    s[...] = run_state.astype(bf16)
    g[...] = run_total
    pl.semaphore_wait(barrier, chips - 1 + 1 + lines - 1 + 3)

    keep, cede = aligned(core, channels // 2), aligned(1 - core, channels // 2)

    def pair(n, src, dst):
        return remote(src, dst, pair_sem.at[0, n], pair_sem.at[1, n], tm=partner)

    pairs_out = [pair(0, g.at[:, cede], pg), pair(1, s.at[:, cede], ps)]
    for copy in pairs_out:
        copy.start()
    for copy in pairs_out:
        copy.wait_recv()

    def ordered(own, others):
        return jnp.where(core == 0, own, others), jnp.where(core == 0, others, own)

    first_s, second_s = ordered(s[:, keep].astype(f32), ps[...].astype(f32))
    first_g, second_g = ordered(g[:, keep], pg[...])
    sf[...] = first_s
    gf[...] = first_g
    gc[...] = first_g * second_g
    sc[...] = (first_s * second_g + second_s).astype(bf16)

    def out_s(q):
        return remote(sc.at[rows(q), cols(q)], sin.at[here], s_sem.at[0, q], s_sem.at[1, here], tm=base + 2 * q)

    def out_g(q):
        return remote(gc.at[:, cols(q)], gin.at[here], g_sem.at[0, q], g_sem.at[1, here], tm=base + 2 * q)

    def in_s(q):
        return remote(sc.at[rows(q), cols(q)], sin.at[q], s_sem.at[0, q], s_sem.at[1, q], tm=base + 2 * q)

    def in_g(q):
        return remote(gc.at[:, cols(q)], gin.at[q], g_sem.at[0, q], g_sem.at[1, q], tm=base + 2 * q)

    @pl.loop(0, chips - 1)
    def _(i):
        q = far_first(i)
        out_g(q).start()
        out_s(q).start()

    sin[here] = sc[rows(here), cols(here)]
    gin[here] = gc[:, cols(here)]

    def diagonal(b):
        at = aligned(b, BLOCK)
        scores = lax.dot_general(
            cc[at], bb[at], (((1,), (1,)), ((), ())), preferred_element_type=f32
        )
        causal = iota((BLOCK, BLOCK), 0) >= iota((BLOCK, BLOCK), 1)
        cols_b, cum_b, dt_b = cols_t[at], cums[b], dts[b]
        per = 128 // hdim
        for first_head in range(0, heads, per):
            lanes = slice(first_head * hdim, (first_head + per) * hdim)
            xa_b = xa[at, lanes]
            lane = iota((BLOCK, 128), 1) // hdim
            total = jnp.zeros((BLOCK, 128), f32)
            for i in range(per):
                h = first_head + i
                seg = jnp.where(causal, cols_b[:, h : h + 1] - cum_b[h : h + 1], -jnp.inf)
                mixw = (scores * jnp.exp(seg) * dt_b[h : h + 1]).astype(bf16)
                product = jnp.dot(mixw, xa_b, preferred_element_type=f32)
                total = jnp.where(lane == i, product, total)
            yd[at, lanes] = total

    diagonal(0)

    def step(k, carry):
        state, decay = carry

        @pl.when(k != here)
        def _():
            in_g(k).wait_recv()
            in_s(k).wait_recv()

        pre[k] = state
        dec[k] = decay
        factor = gin[k]
        return state * factor + sin[k].astype(f32), decay * factor

    state, decay = lax.fori_loop(
        0, chips, step, (jnp.zeros((high, wide), f32), jnp.ones((1, wide), f32))
    )
    xt[mine] = state
    xd[mine] = decay

    def line_copies(q, slot):
        device = q * line + place
        return (
            remote(xt.at[slot], xt.at[slot], xt_sem.at[0, q], xt_sem.at[1, slot], tm=device),
            remote(xd.at[slot], xd.at[slot], xd_sem.at[0, q], xd_sem.at[1, slot], tm=device),
        )

    for o in range(1, lines):
        for copy in line_copies(other_line(o), mine):
            copy.start()
    loads[2].wait()
    z[...] = jax.nn.silu(
        jnp.dot(nrm[RIM:], w_z[...], preferred_element_type=f32).astype(bf16).astype(f32)
    )
    for o in range(1, lines):
        for copy in line_copies(other_line(o), other_line(o)):
            copy.wait_recv()
    start = jnp.zeros((high, wide), f32)
    for k in range(lines):
        start = jnp.where(k < mine, start * xd[k] + xt[k], start)

    def final(k, carry):
        back[k] = (start * dec[k] + pre[k]).astype(back.dtype)
        return carry

    lax.fori_loop(0, chips, final, 0)

    def out_b(q):
        return remote(
            back.at[q], hc.at[rows(here), cols(here)], b_sem.at[0, q], b_sem.at[1, here], tm=base + 2 * q
        )

    def in_b(q):
        return remote(
            back.at[q], hc.at[rows(q), cols(q)], b_sem.at[0, q], b_sem.at[1, q], tm=base + 2 * q
        )

    @pl.loop(0, chips - 1)
    def _(i):
        out_b(far_first(i)).start()

    hc[rows(here), cols(here)] = back[here]
    for b in range(1, blocks):
        diagonal(b)

    @pl.loop(1, chips)
    def _(o):
        in_b(other(o)).wait_recv()

    before = hc[...].astype(f32)
    own, others = ordered(before, before * gf[...] + sf[...])
    give[...] = others.astype(bf16)
    pair_back = pair(2, give, got)
    pair_back.start()
    hin[:, keep] = own
    pair_back.wait_recv()
    hin[:, cede] = got[...].astype(f32)
    incoming = hin[...]
    for b in range(blocks):
        hb[b] = incoming.astype(bf16)
        incoming = incoming * totals[b] + states[b]

    share = steps // devices
    half = share // 2
    inner = channels * devices
    hit = iota((heads, channels), 0) == iota((heads, channels), 1) // hdim
    skip = jnp.sum(jnp.where(hit, column(d_skip[...]), 0.0), axis=0, keepdims=True)

    def product(k):
        at = aligned(k, share)
        yoff = jnp.dot(cc[at], hb[k * share // BLOCK], preferred_element_type=f32)
        y = yd[at] + yoff * ec[at] + skip * xa[at].astype(f32)
        gated = y * z[at]
        square = jnp.sum(gated * gated, axis=1, keepdims=True)
        sq[k] = jnp.broadcast_to(square, (share, share)).T[:1]
        scaled = (gated * norm_gain[...]).astype(bf16)
        part[at] = jnp.dot(scaled, w_out[...], preferred_element_type=f32).astype(bf16)

    features = whole.shape[1]
    low, up = pl.ds(0, features // 2), pl.ds(features // 2, features // 2)

    def half_of(k, n):
        return pl.ds(pl.multiple_of(k * share + n * half, half), half)

    def go(n, src, dst, to):
        return remote(src, dst, send.at[n], recv.at[n], head=to)

    def sums(n):
        at = pl.ds(n * half, half)
        base_sem = 12 * n
        return (
            [
                go(base_sem, part.at[half_of(across, n), low], first.at[0, at], right),
                go(base_sem + 1, part.at[half_of(across, n), up], first.at[1, at], left),
                go(base_sem + 2, part.at[half_of(right, n), up], full.at[0, at, up], right),
                go(base_sem + 3, part.at[half_of(left, n), low], full.at[1, at, low], left),
            ],
            [
                go(base_sem + 4, stage.at[0, at], full.at[0, at, low], right),
                go(base_sem + 5, stage.at[1, at], full.at[1, at, up], left),
            ],
        )

    def hides(n):
        own, lefts, rights = half_of(me, n), half_of(left, n), half_of(right, n)
        base_sem = 12 * n
        return (
            [
                go(base_sem + 6, hid.at[own, low], hid.at[own, low], right),
                go(base_sem + 7, hid.at[own, up], hid.at[own, up], left),
                go(base_sem + 8, hid.at[own, up], hid.at[own, up], right),
                go(base_sem + 9, hid.at[own, low], hid.at[own, low], left),
            ],
            [
                go(base_sem + 10, hid.at[lefts, low], hid.at[lefts, low], right),
                go(base_sem + 11, hid.at[rights, up], hid.at[rights, up], left),
            ],
        )

    def sq_copy(to, slot):
        return remote(sq.at[to], sqs.at[slot], sq_sem.at[0, to], sq_sem.at[1, slot], head=to)

    ones, twos = zip(*[sums(n) for n in range(2)])
    threes, fours = zip(*[hides(n) for n in range(2)])
    loads[3].wait()
    product(across)
    product(right)
    ones[0][0].start()
    ones[0][1].start()
    product(left)
    ones[0][2].start()
    ones[0][3].start()
    product(me)
    for to in (right, left, across):
        sq_copy(to, me).start()
    for copy in ones[1][:2]:
        copy.start()
    sqs[me] = sq[me]

    def pass_on(n):
        at = pl.ds(n * half, half)
        for d, k, lanes in ((0, right, low), (1, left, up)):
            ones[n][d].wait_recv()
            value = part[half_of(k, n), lanes].astype(f32) + first[d, at].astype(f32)
            stage[d, at] = value.astype(stage.dtype)
            twos[n][d].start()

    pass_on(0)
    for copy in ones[1][2:]:
        copy.start()
    pass_on(1)
    for frm in (right, left, across):
        sq_copy(frm, frm).wait_recv()
    square = sqs[0]
    for k in range(1, devices):
        square = square + sqs[k]
    scale = lax.rsqrt(jnp.broadcast_to(square, (share, share)).T / inner + 1e-05)
    for n in range(2):
        for copy in ones[n][2:] + twos[n]:
            copy.wait_recv()
        at, own = pl.ds(n * half, half), half_of(me, n)
        own_rim = pl.ds(pl.multiple_of(me * share + n * half + RIM, RIM), half)
        for k in range(features // share):
            lanes = pl.ds(k * share, share)
            total = part[own, lanes].astype(f32)
            total = total + full[0, at, lanes].astype(f32) + full[1, at, lanes].astype(f32)
            u = whole[own_rim, lanes].astype(f32) + emb[:, lanes]
            hid[own, lanes] = (u + scale[n * half : (n + 1) * half] * total).astype(hid.dtype)
        for copy in threes[n]:
            copy.start()
    mix_cols = aligned(me, w_mix.shape[1])

    def finish(at):
        mixed = jnp.dot(hid[at], w_mix[...], preferred_element_type=f32)
        out[at] = hid[at, mix_cols].astype(f32) + mixed

    for n in range(2):
        for copy, following in zip(threes[n][:2], fours[n]):
            copy.wait_recv()
            following.start()
        if n == 0:
            loads[4].wait()
            finish(aligned(me, share))
    for n in range(2):
        for copy in threes[n][2:]:
            copy.wait_recv()
    finish(aligned(left, share))
    finish(aligned(right, share))
    for n in range(2):
        for copy in fours[n]:
            copy.wait_recv()
        finish(half_of(across, n))
    for n in range(2):
        for copy in ones[n] + twos[n] + threes[n] + fours[n]:
            copy.wait_send()
    for to in (right, left, across):
        sq_copy(to, me).wait_send()
    for copy in pairs_out + [pair_back]:
        copy.wait_send()
    for o in range(1, lines):
        for copy in line_copies(other_line(o), mine):
            copy.wait_send()

    @pl.loop(1, chips)
    def _(o):
        q = other(o)
        out_g(q).wait_send()
        out_s(q).wait_send()
        out_b(q).wait_send()


def layer(tms, devices, whole, emb, in_gain, w_x, w_z, w_bc, w_dt, *rest):
    f32, bf16 = jnp.float32, jnp.bfloat16
    w_mix = rest[-1]
    rows, features = whole.shape
    steps, channels, state_n = rows - RIM, w_x.shape[1], w_bc.shape[1] // 2
    heads = w_dt.shape[0]
    blocks = steps // BLOCK
    share = steps // devices
    line = min(LINE, tms)
    lines = tms // line
    high, wide = 16, 128
    chips, kept = line // 2, channels // 2
    while (state_n // high) * (kept // wide) > chips:
        if wide < kept:
            wide *= 2
        else:
            high *= 2
    weights = (w_x, w_z, w_bc, rest[-2], w_mix)
    scratch = [(w.shape, w.dtype) for w in weights] + [
        ((rows, features), bf16),
        ((rows, channels), f32),
        ((rows, 2 * state_n), f32),
        ((steps, channels), bf16),
        ((steps, state_n), bf16),
        ((steps, state_n), bf16),
        ((blocks, heads, BLOCK), f32),
        ((blocks, heads, BLOCK), f32),
        ((steps, 128), f32),
        ((steps, channels), f32),
        ((blocks, state_n, channels), f32),
        ((blocks, 1, channels), f32),
        ((state_n, channels), bf16),
        ((1, channels), f32),
        ((steps, channels), f32),
        ((steps, channels), f32),
        ((state_n, channels), f32),
        ((blocks, state_n, channels), bf16),
        ((steps, features), bf16),
        ((devices, 1, share), f32),
        ((chips, high, wide), bf16),
        ((chips, 1, wide), f32),
        ((chips, high, wide), f32),
        ((chips, 1, wide), f32),
        ((chips, high, wide), bf16),
        ((lines, high, wide), f32),
        ((lines, 1, wide), f32),
        ((steps, features), bf16),
        ((2, share, features // 2), bf16),
        ((2, share, features), bf16),
        ((2, share, features // 2), bf16),
        ((devices, 1, share), f32),
        ((1, kept), f32),
        ((state_n, kept), bf16),
        ((state_n, kept), f32),
        ((1, kept), f32),
        ((1, kept), f32),
        ((state_n, kept), bf16),
        ((state_n, kept), bf16),
        ((state_n, kept), bf16),
        ((state_n, kept), bf16),
    ]
    args = (whole, emb, in_gain, w_x, w_z, w_bc, w_dt) + rest
    return pl.pallas_call(
        functools.partial(layer_kernel, tms, line, (high, wide), devices),
        out_shape=jax.ShapeDtypeStruct((steps, w_mix.shape[1]), f32),
        in_specs=[FAR if any(a is w for w in weights) else VMEM for a in args],
        out_specs=VMEM,
        scratch_shapes=[pltpu.VMEM(shape, kind) for shape, kind in scratch]
        + [
            DMA((2, chips)),
            DMA((2, chips)),
            DMA((2, lines)),
            DMA((2, lines)),
            DMA((2, chips)),
            DMA((24,)),
            DMA((24,)),
            DMA((2, devices)),
            DMA((len(weights),)),
            DMA((2, 3)),
        ],
        compiler_params=pltpu.CompilerParams(collective_id=1, has_side_effects=True),
        name="layer",
    )(*args)


def sinusoid(timestep, width):
    half = width // 2
    freq = jnp.exp(-math.log(10000.0) * jnp.arange(half, dtype=jnp.float32) / half)
    angle = timestep.astype(jnp.float32)[0] * freq
    return jnp.concatenate([jnp.sin(angle), jnp.cos(angle)])


def shards(
    latent,
    timestep,
    in_gain,
    w_x,
    w_z,
    w_bc,
    w_dt,
    conv_x,
    conv_bc,
    dt_bias,
    a_log,
    d_skip,
    norm_gain,
    w_out,
    w_mix,
):
    tms, devices = lax.axis_size("tm"), lax.axis_size("head")
    whole = gather(latent, tms, devices)
    return layer(
        tms,
        devices,
        whole,
        sinusoid(timestep, whole.shape[1])[None, :],
        in_gain[None, :],
        w_x,
        w_z,
        w_bc,
        w_dt.T,
        conv_x,
        conv_bc,
        dt_bias[None, :],
        a_log[None, :],
        d_skip[None, :],
        norm_gain[None, :],
        w_out,
        w_mix,
    ).astype(jnp.bfloat16)


def solution(mesh):
    in_specs = (
        P("tm", "head"),
        P(),
        P(),
        P(None, "head"),
        P(None, "head"),
        P(),
        P(None, "head"),
        P(None, "head"),
        P(),
        P("head"),
        P("head"),
        P("head"),
        P("head"),
        P("head", None),
        P(None, "head"),
    )
    out_specs = P("tm", "head")
    return jax.shard_map(shards, mesh=mesh, in_specs=in_specs, out_specs=out_specs, check_vma=False)
```

```python
import functools
import math

import jax
import jax.numpy as jnp
from jax import lax
from jax.experimental import pallas as pl
from jax.experimental.pallas import tpu as pltpu
from jax.sharding import PartitionSpec as P

BLOCK = 256
RIM = 16
LINE = 32
MESH = pl.DeviceIdType.MESH
VMEM = pl.BlockSpec(memory_space=pltpu.VMEM)
FAR = pl.BlockSpec(memory_space=pl.ANY)
DMA = pltpu.SemaphoreType.DMA


def remote(src, dst, send, recv, **device):
    return pltpu.make_async_remote_copy(
        src_ref=src, dst_ref=dst, send_sem=send, recv_sem=recv, device_id=device, device_id_type=MESH
    )


def greet(devices, count):
    barrier = pltpu.get_barrier_semaphore()
    for device in devices:
        pl.semaphore_signal(barrier, inc=1, device_id=device, device_id_type=MESH)
    pl.semaphore_wait(barrier, count)


def aligned(index, size):
    return pl.ds(pl.multiple_of(index * size, size), size)


def gather_kernel(tms, heads, lat, out, own_sem, send, recv, rim_send, rim_recv):
    tm, me = lax.axis_index("tm"), lax.axis_index("head")
    right, left = lax.rem(me + 1, heads), lax.rem(me + heads - 1, heads)
    later, earlier = lax.rem(tm + 1, tms), lax.rem(tm + tms - 1, tms)
    rows, width = lat.shape
    half = rows // 2
    greet(
        [{"head": left}, {"head": right}] + [{"tm": earlier, "head": h} for h in range(heads)],
        2 + heads,
    )
    top, bottom = pl.ds(RIM, half), pl.ds(RIM + half, half)
    mine, lefts, rights = aligned(me, width), aligned(left, width), aligned(right, width)

    def own(rows_out, start, sem, to):
        return remote(
            lat.at[pl.ds(start, half)], out.at[rows_out, mine], send.at[sem], recv.at[sem], head=to
        )

    copies = [
        own(top, 0, 0, right),
        own(bottom, half, 1, left),
        own(bottom, half, 2, right),
        own(top, 0, 3, left),
    ]
    for copy in copies[:2]:
        copy.start()
    rims = [
        remote(
            lat.at[pl.ds(rows - RIM, RIM)],
            out.at[pl.ds(0, RIM), mine],
            rim_send.at[h],
            rim_recv.at[me],
            tm=later,
            head=h,
        )
        for h in range(heads)
    ]
    for copy in rims:
        copy.start()
    for copy in copies[2:]:
        copy.start()
    keep = pltpu.make_async_copy(lat, out.at[pl.ds(RIM, rows), mine], own_sem)
    keep.start()
    onward = [
        remote(out.at[top, lefts], out.at[top, lefts], send.at[4], recv.at[4], head=right),
        remote(out.at[bottom, rights], out.at[bottom, rights], send.at[5], recv.at[5], head=left),
    ]
    for copy, following in zip(copies[:2], onward):
        copy.wait_recv()
        following.start()
    for copy in copies[2:] + onward:
        copy.wait_recv()
    for h in range(heads):
        remote(
            lat.at[pl.ds(rows - RIM, RIM)],
            out.at[pl.ds(0, RIM), pl.ds(h * width, width)],
            rim_send.at[h],
            rim_recv.at[h],
            tm=later,
            head=h,
        ).wait_recv()
    for copy in copies + onward + rims:
        copy.wait_send()
    keep.wait()


def gather(lat, tms, heads):
    rows, width = lat.shape
    return pl.pallas_call(
        functools.partial(gather_kernel, tms, heads),
        out_shape=jax.ShapeDtypeStruct((rows + RIM, width * heads), lat.dtype),
        in_specs=[VMEM],
        out_specs=VMEM,
        scratch_shapes=[DMA, DMA((6,)), DMA((6,)), DMA((heads,)), DMA((heads,))],
        compiler_params=pltpu.CompilerParams(
            collective_id=0, has_side_effects=True, vmem_limit_bytes=8 * 2**20
        ),
        cost_estimate=pl.CostEstimate(flops=10**10, bytes_accessed=30 * 2**20, transcendentals=0),
        name="gather_rows",
    )(lat)


def split(value):
    parts = []
    for _ in range(3):
        part = value.astype(jnp.bfloat16)
        parts.append(part)
        value = value - part.astype(jnp.float32)
    return parts


def exact(value, ones):
    total = None
    for part in split(value):
        term = jnp.dot(part, ones, preferred_element_type=jnp.float32)
        total = term if total is None else total + term
    return total


def iota(shape, axis):
    return lax.broadcasted_iota(jnp.int32, shape, axis)


def column(row):
    count = row.shape[1]
    wide = jnp.broadcast_to(row, (count, count))
    return jnp.sum(
        jnp.where(iota((count, count), 0) == iota((count, count), 1), wide, 0.0), axis=1, keepdims=True
    )


def layer_kernel(
    tms,
    line,
    piece,
    devices,
    whole,
    emb,
    in_gain,
    w_x_far,
    w_z_far,
    w_bc_far,
    w_dt,
    conv_x,
    conv_bc,
    dt_bias,
    a_log,
    d_skip,
    norm_gain,
    w_out_far,
    w_mix_far,
    out,
    w_x,
    w_z,
    w_bc,
    w_out,
    w_mix,
    nrm,
    xs,
    bcs,
    xa,
    bb,
    cc,
    cums,
    dts,
    cols_t,
    ec,
    states,
    totals,
    s,
    g,
    yd,
    z,
    hin,
    hb,
    part,
    sq,
    sin,
    gin,
    pre,
    dec,
    back,
    xt,
    xd,
    hid,
    first,
    full,
    stage,
    sqs,
    pg,
    ps,
    sf,
    gf,
    gc,
    sc,
    hc,
    give,
    got,
    s_sem,
    g_sem,
    xt_sem,
    xd_sem,
    b_sem,
    send,
    recv,
    sq_sem,
    w_sem,
    pair_sem,
):
    f32, bf16 = jnp.float32, jnp.bfloat16
    lines = tms // line
    tm = lax.axis_index("tm")
    chips = line // 2
    place, mine = lax.rem(tm, line), tm // line
    here, core = place // 2, lax.rem(place, 2)
    base = mine * line + core
    partner = tm + 1 - 2 * core
    high, wide = piece
    stack = s.shape[0] // high
    me = lax.axis_index("head")
    right, left, across = (lax.rem(me + d, devices) for d in (1, devices - 1, 2))

    def rows(k):
        return aligned(lax.rem(k, stack), high)

    def cols(k):
        return aligned(k // stack, wide)

    def other(o):
        return lax.rem(here + o, chips)

    def other_line(o):
        return lax.rem(mine + o, lines)

    def far_first(i):
        away = (i + 1) // 2
        return other(chips // 2 + jnp.where(lax.rem(i, 2) == 0, away, -away))

    pairs = ((w_x_far, w_x), (w_bc_far, w_bc), (w_z_far, w_z), (w_out_far, w_out), (w_mix_far, w_mix))
    loads = [pltpu.make_async_copy(far, near, w_sem.at[n]) for n, (far, near) in enumerate(pairs)]
    for load in loads:
        load.start()
    barrier = pltpu.get_barrier_semaphore()

    @pl.loop(0, chips - 1)
    def _(i):
        pl.semaphore_signal(barrier, inc=1, device_id={"tm": base + 2 * far_first(i)}, device_id_type=MESH)

    for o in range(1, lines):
        pl.semaphore_signal(
            barrier, inc=1, device_id={"tm": other_line(o) * line + place}, device_id_type=MESH
        )
    pl.semaphore_signal(barrier, inc=1, device_id={"tm": partner}, device_id_type=MESH)
    for device in (left, right, across):
        pl.semaphore_signal(barrier, inc=1, device_id={"head": device}, device_id_type=MESH)

    total_rows = whole.shape[0]
    steps = total_rows - RIM
    chunk = total_rows // 11

    @pl.loop(0, 11)
    def _(c):
        at = aligned(c, chunk)
        u = whole[at].astype(f32) + emb[...]
        mean = jnp.mean(u * u, axis=1, keepdims=True)
        nrm[at] = (u * lax.rsqrt(mean + 1e-05) * in_gain[...]).astype(bf16)

    dt_t = lax.dot_general(
        w_dt[...], nrm[RIM:], (((1,), (1,)), ((), ())), preferred_element_type=f32
    )
    loads[0].wait()
    xs[...] = jnp.dot(nrm[...], w_x[...], preferred_element_type=f32).astype(bf16).astype(f32)
    loads[1].wait()
    bcs[...] = jnp.dot(nrm[...], w_bc[...], preferred_element_type=f32).astype(bf16).astype(f32)

    @pl.when(tm == 0)
    def _():
        xs[:RIM] = jnp.zeros((RIM, xs.shape[1]), f32)
        bcs[:RIM] = jnp.zeros((RIM, bcs.shape[1]), f32)

    taps = conv_x.shape[0]
    state_n = bb.shape[1]
    width = 128

    def conv(source, kernel, c, lanes):
        value = source[pl.ds(pl.multiple_of(c * width + RIM - 8, 8), width + 8), lanes]
        total = jnp.zeros((width, value.shape[1]), f32)
        for k in range(taps):
            at = 8 - taps + 1 + k
            total = total + value[at : at + width] * kernel[k : k + 1, lanes]
        return jax.nn.silu(total).astype(bf16)

    @pl.loop(0, steps // width)
    def _(c):
        at = aligned(c, width)
        for lane in range(0, xs.shape[1], 128):
            lanes = pl.ds(lane, 128)
            xa[at, lanes] = conv(xs, conv_x, c, lanes)
        bb[at] = conv(bcs, conv_bc, c, pl.ds(0, state_n))
        cc[at] = conv(bcs, conv_bc, c, pl.ds(state_n, state_n))

    raw = dt_t + column(dt_bias[...])
    dt_t = jnp.maximum(raw, 0.0) + jnp.log1p(jnp.exp(-jnp.abs(raw)))
    la_t = dt_t * -jnp.exp(column(a_log[...]))
    heads = dt_t.shape[0]
    channels = xa.shape[1]
    hdim = channels // heads
    blocks = steps // BLOCK
    upper = jnp.where(iota((BLOCK, BLOCK), 0) <= iota((BLOCK, BLOCK), 1), 1.0, 0.0).astype(bf16)

    def picks(offset):
        hit = iota((128, channels), 0) == iota((128, channels), 1) // hdim + offset
        return jnp.where(hit, 1.0, 0.0).astype(bf16)

    tail_picks, decay_picks = picks(heads), picks(2 * heads)
    for b in range(blocks):
        span = slice(b * BLOCK, (b + 1) * BLOCK)
        dt_b = dt_t[:, span]
        cum_b = exact(la_t[:, span], upper)
        last = cum_b[:, BLOCK - 1 :]
        tail = jnp.exp(last - cum_b) * dt_b
        cums[b] = cum_b
        dts[b] = dt_b
        pad = jnp.zeros((128 - 3 * heads, BLOCK), f32)
        columns = jnp.concatenate([cum_b, tail, jnp.exp(cum_b), pad], axis=0).T
        cols_t[span] = columns
        ec[span] = exact(columns, decay_picks)
        weighted = (xa[span].astype(f32) * exact(columns, tail_picks)).astype(bf16)
        states[b] = jnp.dot(
            bb[span].astype(f32).T.astype(bf16), weighted, preferred_element_type=f32
        )
        totals[b] = ec[(b + 1) * BLOCK - 1 : (b + 1) * BLOCK]
    run_state, run_total = states[0], totals[0]
    for b in range(1, blocks):
        run_state, run_total = run_state * totals[b] + states[b], run_total * totals[b]
    s[...] = run_state.astype(bf16)
    g[...] = run_total
    pl.semaphore_wait(barrier, chips - 1 + 1 + lines - 1 + 3)

    keep, cede = aligned(core, channels // 2), aligned(1 - core, channels // 2)

    def pair(n, src, dst):
        return remote(src, dst, pair_sem.at[0, n], pair_sem.at[1, n], tm=partner)

    pairs_out = [pair(0, g.at[:, cede], pg), pair(1, s.at[:, cede], ps)]
    for copy in pairs_out:
        copy.start()
    for copy in pairs_out:
        copy.wait_recv()

    def ordered(own, others):
        return jnp.where(core == 0, own, others), jnp.where(core == 0, others, own)

    first_s, second_s = ordered(s[:, keep].astype(f32), ps[...].astype(f32))
    first_g, second_g = ordered(g[:, keep], pg[...])
    sf[...] = first_s
    gf[...] = first_g
    gc[...] = first_g * second_g
    sc[...] = (first_s * second_g + second_s).astype(bf16)

    def out_s(q):
        return remote(sc.at[rows(q), cols(q)], sin.at[here], s_sem.at[0, q], s_sem.at[1, here], tm=base + 2 * q)

    def out_g(q):
        return remote(gc.at[:, cols(q)], gin.at[here], g_sem.at[0, q], g_sem.at[1, here], tm=base + 2 * q)

    def in_s(q):
        return remote(sc.at[rows(q), cols(q)], sin.at[q], s_sem.at[0, q], s_sem.at[1, q], tm=base + 2 * q)

    def in_g(q):
        return remote(gc.at[:, cols(q)], gin.at[q], g_sem.at[0, q], g_sem.at[1, q], tm=base + 2 * q)

    @pl.loop(0, chips - 1)
    def _(i):
        q = far_first(i)
        out_g(q).start()
        out_s(q).start()

    sin[here] = sc[rows(here), cols(here)]
    gin[here] = gc[:, cols(here)]

    def diagonal(b):
        at = aligned(b, BLOCK)
        scores = lax.dot_general(
            cc[at], bb[at], (((1,), (1,)), ((), ())), preferred_element_type=f32
        )
        causal = iota((BLOCK, BLOCK), 0) >= iota((BLOCK, BLOCK), 1)
        cols_b, cum_b, dt_b = cols_t[at], cums[b], dts[b]
        per = 128 // hdim
        for first_head in range(0, heads, per):
            lanes = slice(first_head * hdim, (first_head + per) * hdim)
            xa_b = xa[at, lanes]
            lane = iota((BLOCK, 128), 1) // hdim
            total = jnp.zeros((BLOCK, 128), f32)
            for i in range(per):
                h = first_head + i
                seg = jnp.where(causal, cols_b[:, h : h + 1] - cum_b[h : h + 1], -jnp.inf)
                mixw = (scores * jnp.exp(seg) * dt_b[h : h + 1]).astype(bf16)
                product = jnp.dot(mixw, xa_b, preferred_element_type=f32)
                total = jnp.where(lane == i, product, total)
            yd[at, lanes] = total

    diagonal(0)

    def step(k, carry):
        state, decay = carry

        @pl.when(k != here)
        def _():
            in_g(k).wait_recv()
            in_s(k).wait_recv()

        pre[k] = state
        dec[k] = decay
        factor = gin[k]
        return state * factor + sin[k].astype(f32), decay * factor

    state, decay = lax.fori_loop(
        0, chips, step, (jnp.zeros((high, wide), f32), jnp.ones((1, wide), f32))
    )
    xt[mine] = state
    xd[mine] = decay

    def line_copies(q, slot):
        device = q * line + place
        return (
            remote(xt.at[slot], xt.at[slot], xt_sem.at[0, q], xt_sem.at[1, slot], tm=device),
            remote(xd.at[slot], xd.at[slot], xd_sem.at[0, q], xd_sem.at[1, slot], tm=device),
        )

    for o in range(1, lines):
        for copy in line_copies(other_line(o), mine):
            copy.start()
    loads[2].wait()
    z[...] = jax.nn.silu(
        jnp.dot(nrm[RIM:], w_z[...], preferred_element_type=f32).astype(bf16).astype(f32)
    )
    for o in range(1, lines):
        for copy in line_copies(other_line(o), other_line(o)):
            copy.wait_recv()
    start = jnp.zeros((high, wide), f32)
    for k in range(lines):
        start = jnp.where(k < mine, start * xd[k] + xt[k], start)

    def final(k, carry):
        back[k] = (start * dec[k] + pre[k]).astype(back.dtype)
        return carry

    lax.fori_loop(0, chips, final, 0)

    def out_b(q):
        return remote(
            back.at[q], hc.at[rows(here), cols(here)], b_sem.at[0, q], b_sem.at[1, here], tm=base + 2 * q
        )

    def in_b(q):
        return remote(
            back.at[q], hc.at[rows(q), cols(q)], b_sem.at[0, q], b_sem.at[1, q], tm=base + 2 * q
        )

    @pl.loop(0, chips - 1)
    def _(i):
        out_b(far_first(i)).start()

    hc[rows(here), cols(here)] = back[here]
    for b in range(1, blocks):
        diagonal(b)

    @pl.loop(1, chips)
    def _(o):
        in_b(other(o)).wait_recv()

    before = hc[...].astype(f32)
    own, others = ordered(before, before * gf[...] + sf[...])
    give[...] = others.astype(bf16)
    pair_back = pair(2, give, got)
    pair_back.start()
    hin[:, keep] = own
    pair_back.wait_recv()
    hin[:, cede] = got[...].astype(f32)
    incoming = hin[...]
    for b in range(blocks):
        hb[b] = incoming.astype(bf16)
        incoming = incoming * totals[b] + states[b]

    share = steps // devices
    half = share // 2
    inner = channels * devices
    hit = iota((heads, channels), 0) == iota((heads, channels), 1) // hdim
    skip = jnp.sum(jnp.where(hit, column(d_skip[...]), 0.0), axis=0, keepdims=True)

    def product(k):
        at = aligned(k, share)
        yoff = jnp.dot(cc[at], hb[k * share // BLOCK], preferred_element_type=f32)
        y = yd[at] + yoff * ec[at] + skip * xa[at].astype(f32)
        gated = y * z[at]
        square = jnp.sum(gated * gated, axis=1, keepdims=True)
        sq[k] = jnp.broadcast_to(square, (share, share)).T[:1]
        scaled = (gated * norm_gain[...]).astype(bf16)
        part[at] = jnp.dot(scaled, w_out[...], preferred_element_type=f32).astype(bf16)

    features = whole.shape[1]
    low, up = pl.ds(0, features // 2), pl.ds(features // 2, features // 2)

    def half_of(k, n):
        return pl.ds(pl.multiple_of(k * share + n * half, half), half)

    def go(n, src, dst, to):
        return remote(src, dst, send.at[n], recv.at[n], head=to)

    def sums(n):
        at = pl.ds(n * half, half)
        base_sem = 12 * n
        return (
            [
                go(base_sem, part.at[half_of(across, n), low], first.at[0, at], right),
                go(base_sem + 1, part.at[half_of(across, n), up], first.at[1, at], left),
                go(base_sem + 2, part.at[half_of(right, n), up], full.at[0, at, up], right),
                go(base_sem + 3, part.at[half_of(left, n), low], full.at[1, at, low], left),
            ],
            [
                go(base_sem + 4, stage.at[0, at], full.at[0, at, low], right),
                go(base_sem + 5, stage.at[1, at], full.at[1, at, up], left),
            ],
        )

    def hides(n):
        own, lefts, rights = half_of(me, n), half_of(left, n), half_of(right, n)
        base_sem = 12 * n
        return (
            [
                go(base_sem + 6, hid.at[own, low], hid.at[own, low], right),
                go(base_sem + 7, hid.at[own, up], hid.at[own, up], left),
                go(base_sem + 8, hid.at[own, up], hid.at[own, up], right),
                go(base_sem + 9, hid.at[own, low], hid.at[own, low], left),
            ],
            [
                go(base_sem + 10, hid.at[lefts, low], hid.at[lefts, low], right),
                go(base_sem + 11, hid.at[rights, up], hid.at[rights, up], left),
            ],
        )

    def sq_copy(to, slot):
        return remote(sq.at[to], sqs.at[slot], sq_sem.at[0, to], sq_sem.at[1, slot], head=to)

    ones, twos = zip(*[sums(n) for n in range(2)])
    threes, fours = zip(*[hides(n) for n in range(2)])
    loads[3].wait()
    product(across)
    product(right)
    ones[0][0].start()
    ones[0][1].start()
    product(left)
    ones[0][2].start()
    ones[0][3].start()
    product(me)
    for to in (right, left, across):
        sq_copy(to, me).start()
    for copy in ones[1][:2]:
        copy.start()
    sqs[me] = sq[me]

    def pass_on(n):
        at = pl.ds(n * half, half)
        for d, k, lanes in ((0, right, low), (1, left, up)):
            ones[n][d].wait_recv()
            value = part[half_of(k, n), lanes].astype(f32) + first[d, at].astype(f32)
            stage[d, at] = value.astype(stage.dtype)
            twos[n][d].start()

    pass_on(0)
    for copy in ones[1][2:]:
        copy.start()
    pass_on(1)
    for frm in (right, left, across):
        sq_copy(frm, frm).wait_recv()
    square = sqs[0]
    for k in range(1, devices):
        square = square + sqs[k]
    scale = lax.rsqrt(jnp.broadcast_to(square, (share, share)).T / inner + 1e-05)
    for n in range(2):
        for copy in ones[n][2:] + twos[n]:
            copy.wait_recv()
        at, own = pl.ds(n * half, half), half_of(me, n)
        own_rim = pl.ds(pl.multiple_of(me * share + n * half + RIM, RIM), half)
        for k in range(features // share):
            lanes = pl.ds(k * share, share)
            total = part[own, lanes].astype(f32)
            total = total + full[0, at, lanes].astype(f32) + full[1, at, lanes].astype(f32)
            u = whole[own_rim, lanes].astype(f32) + emb[:, lanes]
            hid[own, lanes] = (u + scale[n * half : (n + 1) * half] * total).astype(hid.dtype)
        for copy in threes[n]:
            copy.start()
    mix_cols = aligned(me, w_mix.shape[1])

    def finish(at):
        mixed = jnp.dot(hid[at], w_mix[...], preferred_element_type=f32)
        out[at] = hid[at, mix_cols].astype(f32) + mixed

    for n in range(2):
        for copy, following in zip(threes[n][:2], fours[n]):
            copy.wait_recv()
            following.start()
        if n == 0:
            loads[4].wait()
            finish(aligned(me, share))
    for n in range(2):
        for copy in threes[n][2:]:
            copy.wait_recv()
    finish(aligned(left, share))
    finish(aligned(right, share))
    for n in range(2):
        for copy in fours[n]:
            copy.wait_recv()
        finish(half_of(across, n))
    for n in range(2):
        for copy in ones[n] + twos[n] + threes[n] + fours[n]:
            copy.wait_send()
    for to in (right, left, across):
        sq_copy(to, me).wait_send()
    for copy in pairs_out + [pair_back]:
        copy.wait_send()
    for o in range(1, lines):
        for copy in line_copies(other_line(o), mine):
            copy.wait_send()

    @pl.loop(1, chips)
    def _(o):
        q = other(o)
        out_g(q).wait_send()
        out_s(q).wait_send()
        out_b(q).wait_send()


def layer(tms, devices, whole, emb, in_gain, w_x, w_z, w_bc, w_dt, *rest):
    f32, bf16 = jnp.float32, jnp.bfloat16
    w_mix = rest[-1]
    rows, features = whole.shape
    steps, channels, state_n = rows - RIM, w_x.shape[1], w_bc.shape[1] // 2
    heads = w_dt.shape[0]
    blocks = steps // BLOCK
    share = steps // devices
    line = min(LINE, tms)
    lines = tms // line
    high, wide = 16, 128
    chips, kept = line // 2, channels // 2
    while (state_n // high) * (kept // wide) > chips:
        if wide < kept:
            wide *= 2
        else:
            high *= 2
    weights = (w_x, w_z, w_bc, rest[-2], w_mix)
    scratch = [(w.shape, w.dtype) for w in weights] + [
        ((rows, features), bf16),
        ((rows, channels), f32),
        ((rows, 2 * state_n), f32),
        ((steps, channels), bf16),
        ((steps, state_n), bf16),
        ((steps, state_n), bf16),
        ((blocks, heads, BLOCK), f32),
        ((blocks, heads, BLOCK), f32),
        ((steps, 128), f32),
        ((steps, channels), f32),
        ((blocks, state_n, channels), f32),
        ((blocks, 1, channels), f32),
        ((state_n, channels), bf16),
        ((1, channels), f32),
        ((steps, channels), f32),
        ((steps, channels), f32),
        ((state_n, channels), f32),
        ((blocks, state_n, channels), bf16),
        ((steps, features), bf16),
        ((devices, 1, share), f32),
        ((chips, high, wide), bf16),
        ((chips, 1, wide), f32),
        ((chips, high, wide), f32),
        ((chips, 1, wide), f32),
        ((chips, high, wide), bf16),
        ((lines, high, wide), f32),
        ((lines, 1, wide), f32),
        ((steps, features), bf16),
        ((2, share, features // 2), bf16),
        ((2, share, features), bf16),
        ((2, share, features // 2), bf16),
        ((devices, 1, share), f32),
        ((1, kept), f32),
        ((state_n, kept), bf16),
        ((state_n, kept), f32),
        ((1, kept), f32),
        ((1, kept), f32),
        ((state_n, kept), bf16),
        ((state_n, kept), bf16),
        ((state_n, kept), bf16),
        ((state_n, kept), bf16),
    ]
    args = (whole, emb, in_gain, w_x, w_z, w_bc, w_dt) + rest
    return pl.pallas_call(
        functools.partial(layer_kernel, tms, line, (high, wide), devices),
        out_shape=jax.ShapeDtypeStruct((steps, w_mix.shape[1]), f32),
        in_specs=[FAR if any(a is w for w in weights) else VMEM for a in args],
        out_specs=VMEM,
        scratch_shapes=[pltpu.VMEM(shape, kind) for shape, kind in scratch]
        + [
            DMA((2, chips)),
            DMA((2, chips)),
            DMA((2, lines)),
            DMA((2, lines)),
            DMA((2, chips)),
            DMA((24,)),
            DMA((24,)),
            DMA((2, devices)),
            DMA((len(weights),)),
            DMA((2, 3)),
        ],
        compiler_params=pltpu.CompilerParams(
            collective_id=1, has_side_effects=True, vmem_limit_bytes=32 * 2**20
        ),
        name="layer",
    )(*args)


def sinusoid(timestep, width):
    half = width // 2
    freq = jnp.exp(-math.log(10000.0) * jnp.arange(half, dtype=jnp.float32) / half)
    angle = timestep.astype(jnp.float32)[0] * freq
    return jnp.concatenate([jnp.sin(angle), jnp.cos(angle)])


def shards(
    latent,
    timestep,
    in_gain,
    w_x,
    w_z,
    w_bc,
    w_dt,
    conv_x,
    conv_bc,
    dt_bias,
    a_log,
    d_skip,
    norm_gain,
    w_out,
    w_mix,
):
    tms, devices = lax.axis_size("tm"), lax.axis_size("head")
    whole = gather(latent, tms, devices)
    return layer(
        tms,
        devices,
        whole,
        sinusoid(timestep, whole.shape[1])[None, :],
        in_gain[None, :],
        w_x,
        w_z,
        w_bc,
        w_dt.T,
        conv_x,
        conv_bc,
        dt_bias[None, :],
        a_log[None, :],
        d_skip[None, :],
        norm_gain[None, :],
        w_out,
        w_mix,
    ).astype(jnp.bfloat16)


def solution(mesh):
    in_specs = (
        P("tm", "head"),
        P(),
        P(),
        P(None, "head"),
        P(None, "head"),
        P(),
        P(None, "head"),
        P(None, "head"),
        P(),
        P("head"),
        P("head"),
        P("head"),
        P("head"),
        P("head", None),
        P(None, "head"),
    )
    out_specs = P("tm", "head")
    return jax.shard_map(shards, mesh=mesh, in_specs=in_specs, out_specs=out_specs, check_vma=False)
```
